128 devices in a mesh: space: 8 (over x_hi, z), rep: 16 (over y, x_lo, core).
Axes of the slice: x: 4 (x_hi: 2, x_lo: 2; x = x_hi * 2 + x_lo), y: 4, z: 4, core: 2. Of those that a mesh axis runs over, the one named last changes fastest.
Arguments:
- features: bfloat16 [16, 40, 96, 1024], P('rep', 'space'), may hold values from -4 to 4.5
- labels: int32 [16, 40, 96], P('rep', 'space'), may hold values from 0 to 2
- w_in: bfloat16 [29, 1024, 256], replicated, may hold values from -0.0625 to 0.0625
- w_proj: bfloat16 [1280, 256], replicated, may hold values from -0.15625 to 0.15625
- w_cls: bfloat16 [256, 3], replicated, may hold values from -0.375 to 0.375
- class_weight: float32 [3], replicated, may hold values from 0.5 to 4
- matching: int32 [16], replicated, may hold values from 0 to 15, as said below
Outputs:
- avg_in: float32 [16, 29696, 256], P('rep', 'space')
- avg_proj: float32 [16, 1280, 256], P('rep', 'space')
- avg_cls: float32 [16, 256, 3], P('rep', 'space')
The draws below stay inside these ranges and needn't reach their ends.
Inputs may be any that keep to these rules, and one draw needn't show every extreme that they name: matching[i] = i XOR matching[0] with matching[0] nonzero, so replicas are matched in pairs.
All inputs are finite; a program needn't handle non-finite values.
Results may differ from the reference program's by a relative error of at most 0.025.
The reference program's roundings to bfloat16 on the way count: a program that leaves them out, or rounds other values in their place, can miss the bound.
Values may be sent and summed in bfloat16 or wider, within the bound.
A program may use at most 256 MiB of HBM per device.

```python
import math
import jax
import jax.numpy as jnp
from jax import lax

COLS = 96
C_IN = 1024
C_OUT = 256
CLS = 3
ROWS = 40
REPLICAS = 16
N_SPACE = 8


def draw_features(key, part):
    key_noise = jax.random.fold_in(key, 11)
    key_level = jax.random.fold_in(key, 12)
    shape = (REPLICAS, ROWS, COLS, C_IN)
    position = jnp.arange(ROWS, dtype=jnp.float32) / max(ROWS - 1, 1)
    level = jax.random.uniform(key_level, (REPLICAS, 1, 1, C_IN), jnp.float32, 0.03, 0.12)
    noise = jnp.clip(2.0 * jax.random.normal(key_noise, shape, jnp.float32), -4.0, 4.0)
    ramp = 1.0 + 2.0 * position
    return (noise + level * ramp[None, :, None, None]).astype(jnp.bfloat16)


def draw_matching(key, part):
    pair_bits = jax.random.randint(jax.random.fold_in(key, 21), (), 1, REPLICAS, dtype=jnp.int32)
    return jnp.bitwise_xor(jnp.arange(REPLICAS, dtype=jnp.int32), pair_bits)


def set_ends(result, rng, low, top_value):
    shape = result.shape
    index_at = [jax.random.randint(jax.random.fold_in(rng, axis), (), 0, shape[axis]) for axis in range(len(shape))]
    result = result.at[tuple(index_at)].set(low)
    longest = shape.index(max(shape))
    index_at[longest] = (index_at[longest] + 1) % shape[longest]
    return result.at[tuple(index_at)].set(top_value)


def scatter_about(rng, shape, width, bound, kind=jnp.bfloat16):
    values = width * jax.random.normal(rng, shape, jnp.float32)
    return jnp.clip(values, min=-bound, max=bound).astype(kind)


def setup_inputs(seed: int = 0) -> dict:
    seeds = jax.random.split(jax.random.key(seed), 8)
    features = draw_features(jax.random.fold_in(seeds[7], 71), 0)
    labels = set_ends(jax.random.randint(seeds[1], (REPLICAS, ROWS, COLS), 0, CLS), jax.random.fold_in(seeds[1], 1), 0, CLS - 1).astype(jnp.int32)
    w_in = scatter_about(seeds[2], (29, C_IN, C_OUT), (9 * C_IN) ** -0.5, 0.0625)
    w_proj = scatter_about(seeds[3], (5 * C_OUT, C_OUT), (5 * C_OUT) ** -0.5, 0.15625)
    w_cls = scatter_about(seeds[4], (C_OUT, CLS), C_OUT ** -0.5, 0.375)
    class_weight = jnp.clip(jnp.exp(jax.random.uniform(seeds[5], (CLS,), jnp.float32, math.log(0.5), math.log(4.0))), 0.5, 4.0)
    matching = draw_matching(jax.random.fold_in(seeds[7], 71), 0)
    return dict(features=features, labels=labels, w_in=w_in, w_proj=w_proj, w_cls=w_cls, class_weight=class_weight, matching=matching)


loss_scale = 1024.0


def shifted(values, offset, along):
    length = values.shape[along]
    extent = abs(offset)
    if extent >= length:
        return jnp.zeros_like(values)
    padding = [(0, 0)] * values.ndim
    padding[along] = (extent, extent)
    return lax.slice_in_dim(jnp.pad(values, padding), extent + offset, extent + offset + length, axis=along)


def block_terms(left, right):
    a = left.reshape(N_SPACE, -1, left.shape[-1]).astype(jnp.float32)
    b = right.reshape(N_SPACE, -1, right.shape[-1]).astype(jnp.float32)
    partial_value = jnp.einsum("spc,spo->sco", a, b, precision=lax.Precision.HIGHEST).astype(jnp.bfloat16)
    return jnp.sum(partial_value.astype(jnp.float32), axis=0)


def one_replica(inputs, w_in, w_proj, w_cls, class_weight):
    field_map, label_map = inputs
    height, col_count, in_width = field_map.shape
    out_width = w_proj.shape[1]
    pixels = height * col_count
    flat_rows = field_map.reshape(pixels, in_width)
    mean_in = (jnp.sum(field_map, axis=(0, 1), dtype=jnp.float32) / pixels).astype(jnp.bfloat16)
    pre_list = [jnp.dot(flat_rows, w_in[0], preferred_element_type=jnp.float32)]
    for k in range(1, 4):
        dilation = 12 * k
        pre_act = jnp.zeros((height, col_count, out_width), jnp.float32)
        for i in range(3):
            row_block = shifted(field_map, (i - 1) * dilation, 0).reshape(pixels, in_width)
            for j in range(3):
                product = jnp.dot(row_block, w_in[1 + 9 * (k - 1) + 3 * i + j], preferred_element_type=jnp.float32)
                pre_act = pre_act + shifted(product.reshape(height, col_count, out_width), (j - 1) * dilation, 1)
        pre_list.append(pre_act.reshape(pixels, out_width))
    pool_pre = jnp.dot(mean_in[None, :], w_in[28], preferred_element_type=jnp.float32)
    act_list = [jax.nn.relu(p).astype(jnp.bfloat16) for p in pre_list]
    pool_act = jnp.broadcast_to(jax.nn.relu(pool_pre).astype(jnp.bfloat16), (pixels, out_width))
    concat = jnp.concatenate(act_list + [pool_act], axis=1)
    y_pre = jnp.dot(concat, w_proj, preferred_element_type=jnp.float32)
    y_act = jax.nn.relu(y_pre).astype(jnp.bfloat16)
    logits = jnp.dot(y_act, w_cls, preferred_element_type=jnp.float32)
    exp_logits = jnp.exp(logits)
    softmax_out = exp_logits / jnp.sum(exp_logits, axis=1, keepdims=True)
    onehot = (label_map.reshape(pixels)[:, None] == jnp.arange(logits.shape[1], dtype=jnp.int32)[None, :]).astype(jnp.float32)
    weight = jnp.sum(onehot * class_weight[None, :], axis=1)
    d_logits = ((softmax_out - onehot) * weight[:, None] * (loss_scale / pixels)).astype(jnp.bfloat16)
    g_cls = block_terms(y_act, d_logits)
    d_y = (jnp.dot(d_logits, w_cls.T, preferred_element_type=jnp.float32) * (y_pre > 0)).astype(jnp.bfloat16)
    g_proj = block_terms(concat, d_y)
    d_cat = jnp.dot(d_y, w_proj.T, preferred_element_type=jnp.float32)
    grad_list = []
    d_first = (d_cat[:, :out_width] * (pre_list[0] > 0)).astype(jnp.bfloat16)
    grad_list.append(block_terms(flat_rows, d_first))
    for k in range(1, 4):
        dilation = 12 * k
        d_branch = (d_cat[:, k * out_width:(k + 1) * out_width] * (pre_list[k] > 0)).astype(jnp.bfloat16)
        d_branch = d_branch.reshape(height, col_count, out_width)
        for i in range(3):
            row_block = shifted(field_map, (i - 1) * dilation, 0)
            for j in range(3):
                grad_list.append(block_terms(row_block, shifted(d_branch, -(j - 1) * dilation, 1)))
    pool_grad = d_cat[:, 4 * out_width:] * (pool_pre > 0)
    s_pool = jnp.sum(pool_grad.reshape(N_SPACE, -1, out_width), axis=1)
    partial_value = (mean_in.astype(jnp.float32)[None, :, None] * s_pool[:, None, :]).astype(jnp.bfloat16)
    grad_list.append(jnp.sum(partial_value.astype(jnp.float32), axis=0))
    g_in = jnp.stack(grad_list).reshape(-1, out_width)
    return (g_in.astype(jnp.bfloat16), g_proj.astype(jnp.bfloat16), g_cls.astype(jnp.bfloat16))


def reference(features, labels, w_in, w_proj, w_cls, class_weight, matching):
    g_in, g_proj, g_cls = lax.map(lambda inputs: one_replica(inputs, w_in, w_proj, w_cls, class_weight), (features, labels))

    def average(grad):
        return (grad.astype(jnp.float32) + grad[matching].astype(jnp.float32)) * 0.5

    return (average(g_in), average(g_proj), average(g_cls))
```

```python
import functools

import jax
import jax.numpy as jnp
from jax import lax
from jax.experimental import pallas as pl
from jax.experimental.pallas import tpu as pltpu
from jax.sharding import PartitionSpec as P

MESH = pl.DeviceIdType.MESH
F32 = jnp.float32
BF16 = jnp.bfloat16

NS = 8
ROWS_DEV = 5
ROWS = 40
COLS = 96
CIN = 1024
COUT = 256
PIX = ROWS_DEV * COLS
FIELD = ROWS * COLS
TAPS = 28
SHARE = 29 * CIN // NS
PROJ_SHARE = 5 * COUT // NS
CLS_SHARE = COUT // NS
OUT_ROWS = SHARE + PROJ_SHARE + CLS_SHARE
PAD = 36
VMEM_LIMIT = 60 * 2**20
loss_scale = 1024.0


def dot(a, b, dims=((1,), (0,))):
    return lax.dot_general(a, b, (dims, ((), ())), preferred_element_type=F32)


def space_barrier(targets):
    barrier = pltpu.get_barrier_semaphore()
    for t in targets:
        pl.semaphore_signal(barrier, inc=1, device_id={"space": t}, device_id_type=MESH)
    pl.semaphore_wait(barrier, len(targets))


def gather_field(x_ref, xf, ssem, rsem):
    me = lax.axis_index("space")
    core = lax.rem(lax.axis_index("rep"), 2)
    xh, z = me // 4, lax.rem(me, 4)

    def idx(x, zz):
        return x * 4 + lax.rem(zz + 8, 4)

    xo = 1 - xh
    X, ZP, ZM = idx(xo, z), idx(xh, z + 1), idx(xh, z - 1)
    way = 1 - 2 * core

    def part(block, half):
        return pl.ds(block * ROWS_DEV, 3) if half == 0 else pl.ds(block * ROWS_DEV + 3, 2)

    def message(m, block, half, target, own=False):
        rows = part(block, half)
        src = x_ref.at[pl.ds(0, 3) if half == 0 else pl.ds(3, 2)] if own else xf.at[rows]
        return pltpu.make_async_remote_copy(
            src, xf.at[rows], ssem.at[m], rsem.at[m], device_id={"space": target}, device_id_type=MESH
        )

    me_blk = idx(xh, z)
    out = {}

    def send(m, *args, **kw):
        out[m] = message(m, *args, **kw)
        out[m].start()

    def arrived(m, half):
        message(m, landing[m], half, X).wait_recv()

    landing = {
        0: idx(xo, z),
        1: idx(xh, z - 1),
        2: idx(xh, z + 1),
        3: idx(xh, z - 1),
        4: idx(xh, z + 1),
        5: idx(xo, z),
        6: idx(xo, z - 1),
        7: idx(xo, z + 1),
        8: idx(xh, z + 2),
        9: idx(xo, z - 1),
        10: idx(xo, z + 1),
        11: idx(xh, z + 2),
        12: idx(xo, z + 2),
        13: idx(xo, z + 2),
    }
    space_barrier([X, ZP, ZM])
    send(0, me_blk, 0, X, own=True)
    send(1, me_blk, 1, ZP, own=True)
    send(2, me_blk, 1, ZM, own=True)
    send(3, me_blk, 0, ZP, own=True)
    send(4, me_blk, 0, ZM, own=True)
    send(5, me_blk, 1, X, own=True)
    xf[pl.ds(me_blk * ROWS_DEV, ROWS_DEV)] = x_ref[...]
    arrived(1, 1)
    send(6, idx(xh, z - 1), 1, X)
    arrived(2, 1)
    send(7, idx(xh, z + 1), 1, X)
    send(8, idx(xh, z - way), 1, idx(xh, z + way))
    arrived(0, 0)
    send(9, idx(xo, z), 0, ZP)
    send(10, idx(xo, z), 0, ZM)
    arrived(3, 0)
    send(11, idx(xh, z - 1), 0, ZP)
    arrived(10, 0)
    send(12, idx(xo, z + 1), 0, ZM)
    arrived(8, 1)
    send(13, idx(xh, z + 2), 1, X)
    arrived(4, 0)
    arrived(9, 0)
    arrived(11, 0)
    arrived(12, 0)
    arrived(5, 1)
    arrived(6, 1)
    arrived(7, 1)
    arrived(13, 1)
    for m in range(14):
        out[m].wait_send()


def transpose_field(xf, xt):
    @pl.loop(0, ROWS // 4)
    def _(c):
        v = xf[pl.ds(c * 4, 4)].reshape(4 * COLS, CIN)
        xt[:, pl.ds(pl.multiple_of(c * (4 * COLS), 128), 4 * COLS)] = v.T


def field_mean(xf):
    def add(r, total):
        v = xf[r].astype(F32)
        return total + jnp.sum(v.reshape(COLS // 8, 8, CIN), axis=0)

    total = lax.fori_loop(0, ROWS, add, jnp.zeros((8, CIN), F32))
    return (jnp.sum(total, axis=0, keepdims=True) / FIELD).astype(BF16)


def forward(xf, w, acc, xs):
    me = lax.axis_index("space")
    base = me * ROWS_DEV
    own = xf[pl.ds(base, ROWS_DEV)].reshape(PIX, CIN)
    acc[0] = dot(own, w[0])
    for k in range(1, 4):
        acc[k] = jnp.zeros((PIX, COUT), F32)
        reach = 12 * k

        @pl.loop(0, 3)
        def _(a, k=k, reach=reach):
            start = base + (a - 1) * reach
            valid = jnp.logical_and(start + ROWS_DEV > 0, start < ROWS)

            @pl.when(valid)
            def _():
                for j in range(ROWS_DEV):
                    r = start + j
                    inside = jnp.logical_and(r >= 0, r < ROWS)
                    rc = jnp.clip(r, 0, ROWS - 1)
                    row = xf[rc]
                    xs[j * COLS : (j + 1) * COLS, :] = jnp.where(inside, row, jnp.zeros_like(row))
                for b in range(3):
                    p = dot(xs[...], w[1 + 9 * (k - 1) + 3 * a + b])
                    for j in range(ROWS_DEV):
                        lo, hi = j * COLS, (j + 1) * COLS
                        if b == 1:
                            acc[k, lo:hi, :] += p[lo:hi]
                        elif b == 0:
                            acc[k, lo + reach : hi, :] += p[lo : hi - reach]
                        else:
                            acc[k, lo : hi - reach, :] += p[lo + reach : hi]


def head(acc, mean, w_pool, lab_ref, wp, wc, cw, d_out, gp_out, gc_out, sp_out):
    pool_pre = dot(jnp.broadcast_to(mean, (16, CIN)), w_pool)[0:1]
    pool_act = jnp.broadcast_to(jax.nn.relu(pool_pre).astype(BF16), (PIX, COUT))
    acts = [jax.nn.relu(acc[k]).astype(BF16) for k in range(4)] + [pool_act]
    y_pre = dot(acts[0], wp[0:COUT])
    for k in range(1, 5):
        y_pre = y_pre + dot(acts[k], wp[k * COUT : (k + 1) * COUT])
    y_act = jax.nn.relu(y_pre).astype(BF16)
    logits = dot(y_act, wc[...])
    lane = lax.broadcasted_iota(jnp.int32, (PIX, 128), 1)
    exp_logits = jnp.where(lane < 3, jnp.exp(logits), 0.0)
    prob = exp_logits / jnp.sum(exp_logits, axis=1, keepdims=True)
    onehot = jnp.where(lane == lab_ref[...], 1.0, 0.0)
    weight = jnp.sum(onehot * cw[...], axis=1, keepdims=True)
    d_logits = ((prob - onehot) * weight * (loss_scale / FIELD)).astype(BF16)
    gc_out[...] = dot(y_act, d_logits, ((0,), (0,))).astype(BF16)
    d_y = jnp.where(y_pre > 0, dot(d_logits, wc[...], ((1,), (1,))), 0.0).astype(BF16)
    for k in range(5):
        gp_out[k * COUT : (k + 1) * COUT, :] = dot(acts[k], d_y, ((0,), (0,))).astype(BF16)
    for k in range(4):
        d_cat = dot(d_y, wp[k * COUT : (k + 1) * COUT], ((1,), (1,)))
        d_out[k] = jnp.where(acc[k] > 0, d_cat, 0.0).astype(BF16)
    d_cat = dot(d_y, wp[4 * COUT : 5 * COUT], ((1,), (1,)))
    s_pool = jnp.sum(jnp.where(pool_pre > 0, d_cat, 0.0), axis=0, keepdims=True)
    sp_out[...] = jnp.broadcast_to(s_pool, (8, COUT))


def kernel_a(x_ref, lab_ref, w_ref, wp, wc, cw, xt, d_out, gp_out, gc_out, sp_out, mean_out, xf, w, acc, xs, ssem, rsem, wsem):
    load = pltpu.make_async_copy(w_ref, w, wsem)
    load.start()
    gather_field(x_ref, xf, ssem, rsem)
    transpose_field(xf, xt)
    mean = field_mean(xf)
    mean_out[...] = jnp.broadcast_to(mean.astype(F32), (8, CIN))
    load.wait()
    forward(xf, w, acc, xs)
    head(acc, mean, w[TAPS], lab_ref, wp, wc, cw, d_out, gp_out, gc_out, sp_out)


def branch_of(tap):
    return jnp.where(tap == 0, 0, jnp.minimum((tap - 1) // 9 + 1, 3))


def share_branches(s):
    first, last = (29 * s) // 8, jnp.minimum((29 * s + 28) // 8, TAPS - 1)
    return branch_of(first), branch_of(last)


def exchange_d(d_ref, gp, gc, sp, dbuf, pbuf, cbuf, sbuf, ssem, rsem):
    me = lax.axis_index("space")
    others = [lax.rem(me + i, NS) for i in range(1, NS)]
    space_barrier(others)

    def copies(i, src_dev, t):
        k0, k1 = share_branches(t)
        rows = pl.ds(src_dev * ROWS_DEV, ROWS_DEV)

        def make(j, src, dst):
            return pltpu.make_async_remote_copy(
                src, dst, ssem.at[i, j], rsem.at[i, j], device_id={"space": t}, device_id_type=MESH
            )

        return (
            make(0, d_ref.at[k0], dbuf.at[0, rows]),
            make(1, d_ref.at[k1], dbuf.at[1, rows]),
            make(2, gp.at[pl.ds(t * PROJ_SHARE, PROJ_SHARE)], pbuf.at[src_dev]),
            make(3, gc.at[pl.ds(t * CLS_SHARE, CLS_SHARE)], cbuf.at[src_dev]),
            make(4, sp, sbuf.at[src_dev]),
        )

    for i in range(1, NS):
        t = others[i - 1]
        c = copies(i - 1, me, t)
        k0, k1 = share_branches(t)
        c[0].start()
        pl.when(k1 != k0)(c[1].start)
        c[2].start()
        c[3].start()
        c[4].start()
    k0, k1 = share_branches(me)
    mine = pl.ds(me * ROWS_DEV, ROWS_DEV)
    dbuf[0, mine] = d_ref[k0]
    dbuf[1, mine] = d_ref[k1]
    pbuf[me] = gp[pl.ds(pl.multiple_of(me * PROJ_SHARE, 32), PROJ_SHARE), :]
    cbuf[me] = gc[pl.ds(pl.multiple_of(me * CLS_SHARE, 32), CLS_SHARE), :]
    sbuf[me] = sp[...]
    for i in range(1, NS):
        src_dev = lax.rem(me - i + NS, NS)
        c = copies(i - 1, src_dev, me)
        c[0].wait_recv()
        pl.when(k1 != k0)(c[1].wait_recv)
        c[2].wait_recv()
        c[3].wait_recv()
        c[4].wait_recv()
    for i in range(1, NS):
        t = others[i - 1]
        c = copies(i - 1, me, t)
        kt0, kt1 = share_branches(t)
        c[0].wait_send()
        pl.when(kt1 != kt0)(c[1].wait_send)
        c[2].wait_send()
        c[3].wait_send()
        c[4].wait_send()


def weight_gradient(xt, dbuf, dsh, acc, o_ref):
    me = lax.axis_index("space")
    k0, _ = share_branches(me)
    first = (29 * me) // 8
    last = jnp.minimum((29 * me + 28) // 8, TAPS - 1)
    dsh[0:PAD] = jnp.zeros((PAD, COLS, COUT), BF16)
    dsh[PAD + ROWS :] = jnp.zeros((PAD, COLS, COUT), BF16)

    @pl.loop(0, 5)
    def _(ti):
        tap = first + ti

        @pl.when(tap <= last)
        def _():
            k = branch_of(tap)
            within = tap - 1 - 9 * (k - 1)
            a = jnp.where(k == 0, 1, within // 3)
            b = jnp.where(k == 0, 1, lax.rem(within + 9, 3))
            slot = jnp.where(k == k0, 0, 1)
            for kk in range(1, 4):
                for bb in (0, 2):
                    reach = 12 * kk

                    @pl.when(jnp.logical_and(k == kk, b == bb))
                    def _(bb=bb, reach=reach):
                        @pl.loop(0, ROWS)
                        def _(r):
                            v = dbuf[slot, r].astype(F32)
                            zero = jnp.zeros((reach, COUT), F32)
                            if bb == 0:
                                v = jnp.concatenate([v[reach:], zero], axis=0)
                            else:
                                v = jnp.concatenate([zero, v[: COLS - reach]], axis=0)
                            dsh[PAD + r] = v.astype(BF16)

            @pl.when(b == 1)
            def _():
                @pl.loop(0, ROWS)
                def _(r):
                    dsh[PAD + r] = dbuf[slot, r]

            off = (a - 1) * 12 * k
            lo, hi = jnp.maximum(off, 0), ROWS + jnp.minimum(off, 0)
            c_lo, c_hi = lo // 8, (hi + 7) // 8
            for half in range(2):
                row0 = tap * CIN + half * 512 - SHARE * me

                @pl.when(jnp.logical_and(row0 > -512, row0 < SHARE))
                def _(half=half, row0=row0):
                    acc[...] = jnp.zeros_like(acc)

                    def chunk(c, _):
                        px = pl.ds(pl.multiple_of(c * (8 * COLS), 128), 8 * COLS)
                        dd = dsh[pl.ds(PAD + c * 8 - off, 8)].reshape(8 * COLS, COUT)
                        acc[...] += dot(xt[half * 512 : half * 512 + 512, px], dd)
                        return 0

                    lax.fori_loop(c_lo, c_hi, chunk, 0)
                    for u in range(4):
                        at = row0 + 128 * u

                        @pl.when(jnp.logical_and(at >= 0, at < SHARE))
                        def _(u=u, at=at):
                            o_ref[pl.ds(pl.multiple_of(at, 128), 128), :] = acc[
                                128 * u : 128 * u + 128, :
                            ].astype(BF16)


def finish(o_ref, pbuf, cbuf, sbuf, mean_ref):
    me = lax.axis_index("space")
    total = pbuf[0].astype(F32)
    for s in range(1, NS):
        total = total + pbuf[s].astype(F32)
    o_ref[SHARE : SHARE + PROJ_SHARE, :] = total.astype(BF16)
    total = cbuf[0].astype(F32)
    for s in range(1, NS):
        total = total + cbuf[s].astype(F32)
    total = total.astype(BF16)
    o_ref[SHARE + PROJ_SHARE :, :] = jnp.concatenate([total, total], axis=1)

    @pl.when(me == NS - 1)
    def _():
        column = mean_ref[...].T[:, 0:1]
        total = jnp.zeros((CIN, COUT), F32)
        for s in range(NS):
            total = total + (column * sbuf[s, 0:1, :]).astype(BF16).astype(F32)
        o_ref[SHARE - CIN : SHARE, :] = total.astype(BF16)


def kernel_b(xt, d_ref, gp, gc, sp, mean_ref, o_ref, dbuf, pbuf, cbuf, sbuf, dsh, acc, ssem, rsem):
    exchange_d(d_ref, gp, gc, sp, dbuf, pbuf, cbuf, sbuf, ssem, rsem)
    weight_gradient(xt, dbuf, dsh, acc, o_ref)
    finish(o_ref, pbuf, cbuf, sbuf, mean_ref)


def per_device(features, labels, w_in, w_proj, w_cls, class_weight, matching):
    x = features[0]
    lab = labels.reshape(PIX, 1)
    wc = jnp.pad(w_cls, ((0, 0), (0, 125)))
    cw = jnp.pad(class_weight, (0, 125)).reshape(1, 128)
    vmem = pl.BlockSpec(memory_space=pltpu.VMEM)
    hbm = pl.BlockSpec(memory_space=pl.ANY)
    xt, d, gp, gc, sp, mean = pl.pallas_call(
        kernel_a,
        out_shape=(
            jax.ShapeDtypeStruct((CIN, FIELD), BF16),
            jax.ShapeDtypeStruct((4, PIX, COUT), BF16),
            jax.ShapeDtypeStruct((5 * COUT, COUT), BF16),
            jax.ShapeDtypeStruct((COUT, 128), BF16),
            jax.ShapeDtypeStruct((8, COUT), F32),
            jax.ShapeDtypeStruct((8, CIN), F32),
        ),
        in_specs=[vmem, vmem, hbm, vmem, vmem, vmem],
        out_specs=(vmem,) * 6,
        scratch_shapes=[
            pltpu.VMEM((ROWS, COLS, CIN), BF16),
            pltpu.VMEM((29, CIN, COUT), BF16),
            pltpu.VMEM((4, PIX, COUT), F32),
            pltpu.VMEM((PIX, CIN), BF16),
            pltpu.SemaphoreType.DMA((14,)),
            pltpu.SemaphoreType.DMA((14,)),
            pltpu.SemaphoreType.DMA,
        ],
        compiler_params=pltpu.CompilerParams(collective_id=0, has_side_effects=True, vmem_limit_bytes=VMEM_LIMIT),
        name="gather_forward",
    )(x, lab, w_in, w_proj, wc, cw)
    d = d.reshape(4, ROWS_DEV, COLS, COUT)
    own = pl.pallas_call(
        kernel_b,
        out_shape=jax.ShapeDtypeStruct((OUT_ROWS, COUT), BF16),
        in_specs=[vmem] * 6,
        out_specs=vmem,
        scratch_shapes=[
            pltpu.VMEM((2, ROWS, COLS, COUT), BF16),
            pltpu.VMEM((NS, PROJ_SHARE, COUT), BF16),
            pltpu.VMEM((NS, CLS_SHARE, 128), BF16),
            pltpu.VMEM((NS, 8, COUT), F32),
            pltpu.VMEM((ROWS + 2 * PAD, COLS, COUT), BF16),
            pltpu.VMEM((512, COUT), F32),
            pltpu.SemaphoreType.DMA((NS - 1, 5)),
            pltpu.SemaphoreType.DMA((NS - 1, 5)),
        ],
        compiler_params=pltpu.CompilerParams(collective_id=1, has_side_effects=True, vmem_limit_bytes=VMEM_LIMIT),
        name="exchange_gradient",
    )(xt, d, gp, gc, sp, mean)

    def swap(mask, value):
        pairs = [(r, r ^ mask) for r in range(lax.axis_size("rep"))]
        return lax.ppermute(value, "rep", pairs)

    partner = lax.switch(matching[0] - 1, [functools.partial(swap, m) for m in range(1, 16)], own)
    avg = (own.astype(F32) + partner.astype(F32)) * 0.5
    return (
        avg[None, :SHARE],
        avg[None, SHARE : SHARE + PROJ_SHARE],
        avg[None, SHARE + PROJ_SHARE :, :3],
    )


def solution(mesh):
    return jax.shard_map(
        per_device,
        mesh=mesh,
        in_specs=(P("rep", "space", None, None), P("rep", "space", None), P(), P(), P(), P(), P()),
        out_specs=(P("rep", "space", None), P("rep", "space", None), P("rep", "space", None)),
        check_vma=False,
    )
```

```python
import functools

import jax
import jax.numpy as jnp
from jax import lax
from jax.experimental import pallas as pl
from jax.experimental.pallas import tpu as pltpu
from jax.sharding import PartitionSpec as P

MESH = pl.DeviceIdType.MESH
F32 = jnp.float32
BF16 = jnp.bfloat16

NS = 8
ROWS_DEV = 5
ROWS = 40
COLS = 96
CIN = 1024
COUT = 256
PIX = ROWS_DEV * COLS
FIELD = ROWS * COLS
TAPS = 28
SHARE = 29 * CIN // NS
PROJ_SHARE = 5 * COUT // NS
CLS_SHARE = COUT // NS
OUT_ROWS = SHARE + PROJ_SHARE + CLS_SHARE
PAD = 4
VMEM_LIMIT = 62 * 2**20
loss_scale = 1024.0


def dot(a, b, dims=((1,), (0,))):
    return lax.dot_general(a, b, (dims, ((), ())), preferred_element_type=F32)


def place():
    sp, rep = lax.axis_index("space"), lax.axis_index("rep")
    core = lax.rem(rep, 2)
    return sp // 4, lax.rem(sp, 4), core, rep - core


def device(xh, z, core, rep0):
    return {"space": xh * 4 + lax.rem(z + 8, 4), "rep": rep0 + core}


def block_rows(block, first=0, count=ROWS_DEV):
    return pl.ds(block * ROWS_DEV + first, count)


ORDER = ((1, 0), (3, 0), (2, 0), (1, 1), (3, 1), (2, 1), (0, 1))


def entry_barrier():
    xh, z, core, rep0 = place()
    barrier = pltpu.get_barrier_semaphore()

    def signal(dev):
        pl.semaphore_signal(barrier, inc=1, device_id=dev, device_id_type=MESH)

    for dz, dc in ORDER:
        signal(device(xh, z + dz, jnp.bitwise_xor(core, dc), rep0))

    @pl.when(xh != core)
    def _():
        signal(device(core, z, xh, rep0))

    pl.semaphore_wait(barrier, 7 + jnp.where(xh != core, 1, 0))


def gather_field(x_hbm, lab_ref, xf, lab, ssem, rsem, lsem, while_waiting):
    xh, z, core, rep0 = place()
    way = 1 - 2 * core
    mine = 4 * core + z
    sibling = device(xh, z, 1 - core, rep0)

    def blk(zz, plane=core):
        return plane * 4 + lax.rem(zz + 8, 4)

    def message(m, block, first, count, target):
        rows = block_rows(block, first, count)
        return pltpu.make_async_remote_copy(
            xf.at[rows], xf.at[rows], ssem.at[m], rsem.at[m], device_id=target, device_id_type=MESH
        )

    partner = device(core, z, xh, rep0)
    swap = pltpu.make_async_remote_copy(
        x_hbm, xf.at[block_rows(4 * xh + z)], ssem.at[13], rsem.at[13], device_id=partner, device_id_type=MESH
    )
    swap_in = pltpu.make_async_remote_copy(
        x_hbm, xf.at[block_rows(mine)], ssem.at[13], rsem.at[13], device_id=partner, device_id_type=MESH
    )
    swap_lab = pltpu.make_async_remote_copy(
        lab_ref, lab, ssem.at[14], rsem.at[14], device_id=partner, device_id_type=MESH
    )
    local = pltpu.make_async_copy(x_hbm, xf.at[block_rows(mine)], lsem)

    @pl.when(xh != core)
    def _():
        swap.start()
        swap_lab.start()
        swap_in.wait_recv()
        swap_lab.wait_recv()

    @pl.when(xh == core)
    def _():
        local.start()
        lab[...] = lab_ref[...]
        local.wait()

    out = []

    def send(*args):
        c = message(*args)
        c.start()
        out.append(c)

    def arrived(m, block, first, count):
        message(m, block, first, count, sibling).wait_recv()

    ahead, behind = device(xh, z + way, core, rep0), device(xh, z - way, core, rep0)
    send(0, mine, 0, 3, ahead)
    send(1, mine, 3, 2, behind)
    send(2, mine, 3, 2, ahead)
    send(3, mine, 0, 3, behind)
    send(6, mine, 0, 5, sibling)
    while_waiting(xf)
    arrived(0, blk(z - way), 0, 3)
    send(4, blk(z - way), 0, 3, ahead)
    arrived(1, blk(z + way), 3, 2)
    send(5, blk(z + way), 3, 2, behind)
    send(7, blk(z - way), 0, 3, sibling)
    send(8, blk(z + way), 3, 2, sibling)
    arrived(2, blk(z - way), 3, 2)
    send(9, blk(z - way), 3, 2, sibling)
    arrived(3, blk(z + way), 0, 3)
    send(10, blk(z + way), 0, 3, sibling)
    arrived(5, blk(z + 2), 3, 2)
    send(11, blk(z + 2), 3, 2, sibling)
    arrived(4, blk(z + 2), 0, 3)
    send(12, blk(z + 2), 0, 3, sibling)
    other = 1 - core
    arrived(6, blk(z, other), 0, 5)
    arrived(7, blk(z + way, other), 0, 3)
    arrived(8, blk(z - way, other), 3, 2)
    arrived(9, blk(z + way, other), 3, 2)
    arrived(10, blk(z - way, other), 0, 3)
    arrived(11, blk(z + 2, other), 3, 2)
    arrived(12, blk(z + 2, other), 0, 3)

    def drain():
        for c in out:
            c.wait_send()

        @pl.when(xh != core)
        def _():
            swap.wait_send()
            swap_lab.wait_send()

    return drain


def transpose_field(xf, xt):
    @pl.loop(0, ROWS // 4)
    def _(c):
        v = xf[pl.ds(c * 4, 4)].reshape(4 * COLS, CIN)
        xt[:, pl.ds(pl.multiple_of(c * (4 * COLS), 128), 4 * COLS)] = v.T


def field_mean(xf):
    def add(r, total):
        v = xf[r].astype(F32)
        return total + jnp.sum(v.reshape(COLS // 8, 8, CIN), axis=0)

    total = lax.fori_loop(0, ROWS, add, jnp.zeros((8, CIN), F32))
    return (jnp.sum(total, axis=0, keepdims=True) / FIELD).astype(BF16)


def add_tap(acc, k, b, p, fresh=False):
    reach = 12 * k
    if b == 1:
        acc[k] = p if fresh else acc[k] + p
        return
    for j in range(ROWS_DEV):
        lo, hi = j * COLS, (j + 1) * COLS
        if b == 0:
            acc[k, lo + reach : hi, :] += p[lo : hi - reach]
        else:
            acc[k, lo : hi - reach, :] += p[lo + reach : hi]


def forward_own(xf, w, acc, base):
    own = xf[pl.ds(base, ROWS_DEV)].reshape(PIX, CIN)
    acc[0] = dot(own, w[0])
    for k in range(1, 4):
        for b in (1, 0, 2):
            add_tap(acc, k, b, dot(own, w[1 + 9 * (k - 1) + 3 + b]), fresh=True)


def forward_others(xf, w, acc, xs, base):
    for k in range(1, 4):
        reach = 12 * k

        @pl.loop(0, 2)
        def _(half, k=k, reach=reach):
            a = 2 * half
            start = base + (a - 1) * reach
            valid = jnp.logical_and(start + ROWS_DEV > 0, start < ROWS)

            @pl.when(valid)
            def _():
                for j in range(ROWS_DEV):
                    r = start + j
                    inside = jnp.logical_and(r >= 0, r < ROWS)
                    row = xf[jnp.clip(r, 0, ROWS - 1)]
                    xs[j * COLS : (j + 1) * COLS, :] = jnp.where(inside, row, jnp.zeros_like(row))
                for b in range(3):
                    add_tap(acc, k, b, dot(xs[...], w[1 + 9 * (k - 1) + 3 * a + b]))


def head(acc, mean, w_pool, lab, wp, wc, cw, d_out, gp_out, gc_out, sp_out):
    pool_pre = dot(jnp.broadcast_to(mean, (16, CIN)), w_pool)[0:1]
    pool_act = jnp.broadcast_to(jax.nn.relu(pool_pre).astype(BF16), (PIX, COUT))
    acts = [jax.nn.relu(acc[k]).astype(BF16) for k in range(4)] + [pool_act]
    y_pre = dot(acts[0], wp[0:COUT])
    for k in range(1, 5):
        y_pre = y_pre + dot(acts[k], wp[k * COUT : (k + 1) * COUT])
    y_act = jax.nn.relu(y_pre).astype(BF16)
    logits = dot(y_act, wc[...])
    lane = lax.broadcasted_iota(jnp.int32, (PIX, 128), 1)
    lab_t = lab[...].astype(F32).T
    label = jnp.concatenate([lab_t[:COLS, j : j + 1] for j in range(ROWS_DEV)], axis=0)
    exp_logits = jnp.where(lane < 3, jnp.exp(logits), 0.0)
    prob = exp_logits / jnp.sum(exp_logits, axis=1, keepdims=True)
    onehot = jnp.where(lane.astype(F32) == label, 1.0, 0.0)
    weight = jnp.sum(onehot * cw[...], axis=1, keepdims=True)
    d_logits = ((prob - onehot) * weight * (loss_scale / FIELD)).astype(BF16)
    d_y = jnp.where(y_pre > 0, dot(d_logits, wc[...], ((1,), (1,))), 0.0).astype(BF16)
    for k in range(4):
        d_cat = dot(d_y, wp[k * COUT : (k + 1) * COUT], ((1,), (1,)))
        d_out[k] = jnp.where(acc[k] > 0, d_cat, 0.0).astype(BF16).reshape(ROWS_DEV, COLS, COUT)
    d_cat = dot(d_y, wp[4 * COUT : 5 * COUT], ((1,), (1,)))
    s_pool = jnp.sum(jnp.where(pool_pre > 0, d_cat, 0.0), axis=0, keepdims=True)
    sp_out[...] = jnp.broadcast_to(s_pool, (8, COUT))
    gc_out[...] = dot(y_act, d_logits, ((0,), (0,))).astype(BF16)

    def rest():
        for k in range(5):
            gp_out[k * COUT : (k + 1) * COUT, :] = dot(acts[k], d_y, ((0,), (0,))).astype(BF16)

    return rest


def branch_of(tap):
    return jnp.where(tap == 0, 0, jnp.minimum((tap - 1) // 9 + 1, 3))


def pick(i, values):
    r = jnp.int32(values[-1])
    for j, v in enumerate(values[:-1]):
        r = jnp.where(i == j, v, r)
    return r


def share_taps(s):
    return (29 * s) // 8, jnp.minimum((29 * s + 28) // 8, TAPS - 1)


def row_blocks(slot, last_only=False):
    table = []
    for s in range(NS):
        lo, hi = (29 * s) // 8, min((29 * s + 28) // 8, TAPS - 1)
        bits = 0
        k0 = 0 if lo == 0 else (lo - 1) // 9 + 1
        for t in range(lo, hi + 1):
            k = 0 if t == 0 else (t - 1) // 9 + 1
            if (k != k0) != (slot == 1):
                continue
            a = 1 if k == 0 else (t - 1) % 9 // 3
            off = (a - 1) * 12 * k
            for h in range(ROWS):
                if 0 <= h + off < ROWS:
                    bits |= 1 << (h // ROWS_DEV)
        table.append(bits)
    return table


def wanted(slot, share, block):
    return lax.rem(lax.shift_right_logical(pick(share, row_blocks(slot)), block), 2) == 1


def d_copies(i, src_block, share, target, bufs, sems):
    d, gp, gc, sp, dbuf, pbuf, cbuf, sbuf = bufs
    ssem, rsem = sems
    lo, hi = share_taps(share)

    def make(j, src, dst):
        return pltpu.make_async_remote_copy(
            src, dst, ssem.at[i, j], rsem.at[i, j], device_id=target, device_id_type=MESH
        )

    return (
        make(0, d.at[branch_of(lo)], dbuf.at[0, block_rows(src_block)]),
        make(1, d.at[branch_of(hi)], dbuf.at[1, block_rows(src_block)]),
        make(2, gp.at[pl.ds(share * PROJ_SHARE, PROJ_SHARE)], pbuf.at[src_block]),
        make(3, gc.at[pl.ds(share * CLS_SHARE, CLS_SHARE)], cbuf.at[src_block]),
        make(4, sp, sbuf.at[src_block]),
    )


def shift_block(slot, block, rows_of, dsh):
    _, z, core, _ = place()
    first, last = share_taps(4 * core + z)
    k0 = branch_of(first)

    @pl.loop(0, 5)
    def _(ti):
        tap = first + ti
        k = branch_of(tap)
        b = jnp.where(k == 0, 1, lax.rem(tap + 2, 3))
        uses = jnp.logical_and(tap <= last, (k != k0) == (slot == 1))

        @pl.when(uses)
        def _():
            for kk in range(1, 4):
                reach = 12 * kk
                for bb in (0, 2):

                    @pl.when(jnp.logical_and(k == kk, b == bb))
                    def _(bb=bb, reach=reach):
                        @pl.loop(0, ROWS_DEV)
                        def _(j):
                            v = rows_of(j).astype(F32)
                            zero = jnp.zeros((reach, COUT), F32)
                            if bb == 0:
                                v = jnp.concatenate([v[reach:], zero], axis=0)
                            else:
                                v = jnp.concatenate([zero, v[: COLS - reach]], axis=0)
                            dsh[ti, PAD + block * ROWS_DEV + j] = v.astype(BF16)

            @pl.when(b == 1)
            def _():
                @pl.loop(0, ROWS_DEV)
                def _(j):
                    dsh[ti, PAD + block * ROWS_DEV + j] = rows_of(j)


def weight_gradient(xt, dsh, acc, o_ref):
    _, z, core, _ = place()
    share = 4 * core + z
    first, last = share_taps(share)

    @pl.loop(0, 10)
    def _(step):
        ti, half = step // 2, lax.rem(step, 2)
        tap = first + ti
        row0 = tap * CIN + half * 512 - SHARE * share
        touches = jnp.logical_and(row0 > -512, row0 < SHARE)

        @pl.when(jnp.logical_and(tap <= last, touches))
        def _():
            k = branch_of(tap)
            a = jnp.where(k == 0, 1, lax.rem(tap + 8, 9) // 3)
            off = (a - 1) * 12 * k
            lo, hi = jnp.maximum(off, 0), ROWS + jnp.minimum(off, 0)
            acc[...] = jnp.zeros_like(acc)
            m = pl.ds(pl.multiple_of(half * 512, 512), 512)

            def chunk(c, _):
                px = pl.ds(pl.multiple_of(c * (8 * COLS), 128), 8 * COLS)
                dd = dsh[ti, pl.ds(PAD + c * 8 - off, 8)].reshape(8 * COLS, COUT)
                acc[...] += dot(xt[m, px], dd)
                return 0

            lax.fori_loop(lo // 8, (hi + 7) // 8, chunk, 0)
            for u in range(4):
                at = row0 + 128 * u

                @pl.when(jnp.logical_and(at >= 0, at < SHARE))
                def _(u=u, at=at):
                    o_ref[pl.ds(pl.multiple_of(at, 128), 128), :] = acc[128 * u : 128 * u + 128, :].astype(BF16)


def finish(o_ref, pbuf, cbuf, sbuf, mean_ref, share):
    total = pbuf[0].astype(F32)
    for s in range(1, NS):
        total = total + pbuf[s].astype(F32)
    o_ref[SHARE : SHARE + PROJ_SHARE, :] = total.astype(BF16)
    total = cbuf[0].astype(F32)
    for s in range(1, NS):
        total = total + cbuf[s].astype(F32)
    total = total.astype(BF16)
    o_ref[SHARE + PROJ_SHARE :, :] = jnp.concatenate([total, total], axis=1)

    @pl.when(share == NS - 1)
    def _():
        column = mean_ref[...].T[:, 0:1]
        total = jnp.zeros((CIN, COUT), F32)
        for s in range(NS):
            total = total + (column * sbuf[s, 0:1, :]).astype(BF16).astype(F32)
        o_ref[SHARE - CIN : SHARE, :] = total.astype(BF16)


def kernel(
    x_hbm, lab_ref, w_ref, wp, wc, cw, o_ref,
    xf, w, acc, xs, lab, d, gp, gc, sp, mean_ref, xt, dbuf, pbuf, cbuf, sbuf, dsh, acc_w,
    gs, gr, ds_, dr, lsem, wsem,
):
    xh, z, core, rep0 = place()
    share = 4 * core + z
    base = share * ROWS_DEV
    load = pltpu.make_async_copy(w_ref, w, wsem)
    load.start()
    entry_barrier()

    def while_waiting(xf):
        load.wait()
        forward_own(xf, w, acc, base)
        dsh[:, 0:PAD] = jnp.zeros((5, PAD, COLS, COUT), BF16)
        dsh[:, PAD + ROWS :] = jnp.zeros((5, PAD, COLS, COUT), BF16)

    drain = gather_field(x_hbm, lab_ref, xf, lab, gs, gr, lsem, while_waiting)
    mean = field_mean(xf)
    mean_ref[...] = jnp.broadcast_to(mean.astype(F32), (8, CIN))
    forward_others(xf, w, acc, xs, base)
    rest = head(acc, mean, w[TAPS], lab, wp, wc, cw, d, gp, gc, sp)

    bufs, sems = (d, gp, gc, sp, dbuf, pbuf, cbuf, sbuf), (ds_, dr)
    sent = []
    for i, (dz, dc) in enumerate(ORDER):
        c2 = jnp.bitwise_xor(core, dc)
        z2 = lax.rem(z + dz, 4)
        t = 4 * c2 + z2
        c = d_copies(i, share, t, device(xh, z2, c2, rep0), bufs, sems)
        flags = (wanted(0, t, share), wanted(1, t, share))
        sent.append((c, flags, t))
        pl.when(flags[0])(c[0].start)
        pl.when(flags[1])(c[1].start)
    rest()
    transpose_field(xf, xt)
    for c, _, t in sent:
        c[2].start()
        c[3].start()
        pl.when(t == NS - 1)(c[4].start)

    lo, hi = share_taps(share)
    kb0, kb1 = branch_of(lo), branch_of(hi)
    pl.when(wanted(0, share, share))(lambda: shift_block(0, share, lambda j: d[kb0, j], dsh))
    pl.when(wanted(1, share, share))(lambda: shift_block(1, share, lambda j: d[kb1, j], dsh))

    def source(i):
        dz, dc = pick(i, [o[0] for o in ORDER]), pick(i, [o[1] for o in ORDER])
        c2 = jnp.bitwise_xor(core, dc)
        z2 = lax.rem(z - dz + 4, 4)
        return 4 * c2 + z2, device(xh, z2, c2, rep0)

    @pl.loop(0, NS - 1)
    def _(i):
        block, dev = source(i)
        c = d_copies(i, block, share, dev, bufs, sems)
        for slot in range(2):

            @pl.when(wanted(slot, share, block))
            def _(slot=slot):
                c[slot].wait_recv()
                shift_block(slot, block, lambda j: dbuf[slot, block * ROWS_DEV + j], dsh)

    weight_gradient(xt, dsh, acc_w, o_ref)
    pbuf[share] = gp[pl.ds(pl.multiple_of(share * PROJ_SHARE, 32), PROJ_SHARE), :]
    cbuf[share] = gc[pl.ds(pl.multiple_of(share * CLS_SHARE, 32), CLS_SHARE), :]
    sbuf[share] = sp[...]

    @pl.loop(0, NS - 1)
    def _(i):
        block, dev = source(i)
        c = d_copies(i, block, share, dev, bufs, sems)
        c[2].wait_recv()
        c[3].wait_recv()
        pl.when(share == NS - 1)(c[4].wait_recv)

    finish(o_ref, pbuf, cbuf, sbuf, mean_ref, share)
    drain()
    for c, flags, t in sent:
        pl.when(flags[0])(c[0].wait_send)
        pl.when(flags[1])(c[1].wait_send)
        c[2].wait_send()
        c[3].wait_send()
        pl.when(t == NS - 1)(c[4].wait_send)


def home(device_index, mask):
    sp, rep = device_index // 16, device_index % 16
    xh, z, core = sp // 4, sp % 4, rep % 2
    return (4 * core + z) * 16 + ((rep - core + xh) ^ mask)


def per_device(features, labels, w_in, w_proj, w_cls, class_weight, matching):
    x = features[0]
    lab = jnp.pad(labels[0], ((0, 8 - ROWS_DEV), (0, 128 - COLS)))
    wc = jnp.pad(w_cls, ((0, 0), (0, 125)))
    cw = jnp.pad(class_weight, (0, 125)).reshape(1, 128)
    vmem = pl.BlockSpec(memory_space=pltpu.VMEM)
    hbm = pl.BlockSpec(memory_space=pl.ANY)
    done = pl.pallas_call(
        kernel,
        out_shape=jax.ShapeDtypeStruct((OUT_ROWS, COUT), BF16),
        in_specs=[hbm, vmem, hbm, vmem, vmem, vmem],
        out_specs=vmem,
        scratch_shapes=[
            pltpu.VMEM((ROWS, COLS, CIN), BF16),
            pltpu.VMEM((29, CIN, COUT), BF16),
            pltpu.VMEM((4, PIX, COUT), F32),
            pltpu.VMEM((PIX, CIN), BF16),
            pltpu.VMEM((8, 128), jnp.int32),
            pltpu.VMEM((4, ROWS_DEV, COLS, COUT), BF16),
            pltpu.VMEM((5 * COUT, COUT), BF16),
            pltpu.VMEM((COUT, 128), BF16),
            pltpu.VMEM((8, COUT), F32),
            pltpu.VMEM((8, CIN), F32),
            pltpu.VMEM((CIN, FIELD), BF16),
            pltpu.VMEM((2, ROWS, COLS, COUT), BF16),
            pltpu.VMEM((NS, PROJ_SHARE, COUT), BF16),
            pltpu.VMEM((NS, CLS_SHARE, 128), BF16),
            pltpu.VMEM((NS, 8, COUT), F32),
            pltpu.VMEM((5, ROWS + 2 * PAD, COLS, COUT), BF16),
            pltpu.VMEM((512, COUT), F32),
            pltpu.SemaphoreType.DMA((15,)),
            pltpu.SemaphoreType.DMA((15,)),
            pltpu.SemaphoreType.DMA((NS - 1, 5)),
            pltpu.SemaphoreType.DMA((NS - 1, 5)),
            pltpu.SemaphoreType.DMA,
            pltpu.SemaphoreType.DMA,
        ],
        compiler_params=pltpu.CompilerParams(collective_id=0, has_side_effects=True, vmem_limit_bytes=VMEM_LIMIT),
        name="field_gradient",
    )(x, lab, w_in, w_proj, wc, cw)

    def deliver(mask, value):
        n = lax.axis_size("rep") * lax.axis_size("space")
        own = lax.ppermute(value, ("space", "rep"), [(i, home(i, 0)) for i in range(n)])
        partner = lax.ppermute(value, ("space", "rep"), [(i, home(i, mask)) for i in range(n)])
        return own, partner

    own, partner = lax.switch(matching[0] - 1, [functools.partial(deliver, m) for m in range(1, 16)], done)

    def average(lo, hi, width):
        mean = (own[lo:hi, :width].astype(F32) + partner[lo:hi, :width].astype(F32)) * 0.5
        return mean[None]

    return (
        average(0, SHARE, COUT),
        average(SHARE, SHARE + PROJ_SHARE, COUT),
        average(SHARE + PROJ_SHARE, OUT_ROWS, 3),
    )


def solution(mesh):
    return jax.shard_map(
        per_device,
        mesh=mesh,
        in_specs=(P("rep", "space", None, None), P("rep", "space", None), P(), P(), P(), P(), P()),
        out_specs=(P("rep", "space", None), P("rep", "space", None), P("rep", "space", None)),
        check_vma=False,
    )
```

```python
import functools

import jax
import jax.numpy as jnp
from jax import lax
from jax.experimental import pallas as pl
from jax.experimental.pallas import tpu as pltpu
from jax.sharding import PartitionSpec as P

MESH = pl.DeviceIdType.MESH
F32 = jnp.float32
BF16 = jnp.bfloat16

NS = 8
ROWS_DEV = 5
ROWS = 40
COLS = 96
CIN = 1024
COUT = 256
PIX = ROWS_DEV * COLS
FIELD = ROWS * COLS
TAPS = 28
SHARE = 29 * CIN // NS
PROJ_SHARE = 5 * COUT // NS
CLS_SHARE = COUT // NS
OUT_ROWS = SHARE + PROJ_SHARE + CLS_SHARE
M_TILE = 1024
VMEM_LIMIT = 62 * 2**20
loss_scale = 1024.0


def dot(a, b, dims=((1,), (0,))):
    return lax.dot_general(a, b, (dims, ((), ())), preferred_element_type=F32)


def place():
    sp, rep = lax.axis_index("space"), lax.axis_index("rep")
    core = lax.rem(rep, 2)
    return sp // 4, lax.rem(sp, 4), core, rep - core


def device(xh, z, core, rep0):
    return {"space": xh * 4 + lax.rem(z + 8, 4), "rep": rep0 + core}


def block_rows(block, first=0, count=ROWS_DEV):
    return pl.ds(block * ROWS_DEV + first, count)


ORDER = ((1, 0), (3, 0), (2, 0), (0, 1), (1, 1), (3, 1), (2, 1))


def far_first(z):
    return jnp.where(jnp.logical_or(z == 0, z == 3), 1, 0)


def other_core(dz, late, z_target):
    return jnp.where(dz == 0, 1, jnp.bitwise_xor(late, far_first(z_target)))


def entry_barrier():
    xh, z, core, rep0 = place()
    barrier = pltpu.get_barrier_semaphore()

    def signal(dev):
        pl.semaphore_signal(barrier, inc=1, device_id=dev, device_id_type=MESH)

    for dz, dc in ((1, 0), (2, 0), (3, 0), (0, 1), (1, 1), (2, 1), (3, 1)):
        signal(device(xh, z + dz, jnp.bitwise_xor(core, dc), rep0))

    @pl.when(xh != core)
    def _():
        signal(device(core, z, xh, rep0))

    pl.semaphore_wait(barrier, 7 + jnp.where(xh != core, 1, 0))


def gather_field(x_hbm, lab_ref, xf, lab, ssem, rsem, lsem, while_waiting):
    xh, z, core, rep0 = place()
    way = 1 - 2 * core
    mine = 4 * core + z
    sibling = device(xh, z, 1 - core, rep0)

    def blk(zz, plane=core):
        return plane * 4 + lax.rem(zz + 8, 4)

    def message(m, block, first, count, target):
        rows = block_rows(block, first, count)
        return pltpu.make_async_remote_copy(
            xf.at[rows], xf.at[rows], ssem.at[m], rsem.at[m], device_id=target, device_id_type=MESH
        )

    partner = device(core, z, xh, rep0)
    swap = pltpu.make_async_remote_copy(
        x_hbm, xf.at[block_rows(4 * xh + z)], ssem.at[13], rsem.at[13], device_id=partner, device_id_type=MESH
    )
    swap_in = pltpu.make_async_remote_copy(
        x_hbm, xf.at[block_rows(mine)], ssem.at[13], rsem.at[13], device_id=partner, device_id_type=MESH
    )
    swap_lab = pltpu.make_async_remote_copy(
        lab_ref, lab, ssem.at[14], rsem.at[14], device_id=partner, device_id_type=MESH
    )
    local = pltpu.make_async_copy(x_hbm, xf.at[block_rows(mine)], lsem)

    @pl.when(xh != core)
    def _():
        swap.start()
        swap_lab.start()
        swap_in.wait_recv()
        swap_lab.wait_recv()

    @pl.when(xh == core)
    def _():
        local.start()
        lab[...] = lab_ref[...]
        local.wait()

    out = []

    def send(*args):
        c = message(*args)
        c.start()
        out.append(c)

    def arrived(m, block, first, count):
        message(m, block, first, count, sibling).wait_recv()

    ahead, behind = device(xh, z + way, core, rep0), device(xh, z - way, core, rep0)
    send(0, mine, 0, 3, ahead)
    send(1, mine, 3, 2, behind)
    send(2, mine, 3, 2, ahead)
    send(3, mine, 0, 3, behind)
    send(6, mine, 0, 5, sibling)
    while_waiting(xf)
    arrived(0, blk(z - way), 0, 3)
    send(4, blk(z - way), 0, 3, ahead)
    arrived(1, blk(z + way), 3, 2)
    send(5, blk(z + way), 3, 2, behind)
    send(7, blk(z - way), 0, 3, sibling)
    send(8, blk(z + way), 3, 2, sibling)
    arrived(2, blk(z - way), 3, 2)
    send(9, blk(z - way), 3, 2, sibling)
    arrived(3, blk(z + way), 0, 3)
    send(10, blk(z + way), 0, 3, sibling)
    arrived(5, blk(z + 2), 3, 2)
    send(11, blk(z + 2), 3, 2, sibling)
    arrived(4, blk(z + 2), 0, 3)
    send(12, blk(z + 2), 0, 3, sibling)
    other = 1 - core
    arrived(6, blk(z, other), 0, 5)
    arrived(7, blk(z + way, other), 0, 3)
    arrived(8, blk(z - way, other), 3, 2)
    arrived(9, blk(z + way, other), 3, 2)
    arrived(10, blk(z - way, other), 0, 3)
    arrived(11, blk(z + 2, other), 3, 2)
    arrived(12, blk(z + 2, other), 0, 3)

    def drain():
        for c in out:
            c.wait_send()

        @pl.when(xh != core)
        def _():
            swap.wait_send()
            swap_lab.wait_send()

    return drain


def transpose_field(xf, xt):
    @pl.loop(0, ROWS // 4)
    def _(c):
        v = xf[pl.ds(c * 4, 4)].reshape(4 * COLS, CIN)
        xt[:, pl.ds(pl.multiple_of(c * (4 * COLS), 128), 4 * COLS)] = v.T


def field_mean(xf):
    def add(r, total):
        v = xf[r].astype(F32)
        return total + jnp.sum(v.reshape(COLS // 8, 8, CIN), axis=0)

    total = lax.fori_loop(0, ROWS, add, jnp.zeros((8, CIN), F32))
    return (jnp.sum(total, axis=0, keepdims=True) / FIELD).astype(BF16)


def add_tap(acc, k, b, p, fresh=False):
    reach = 12 * k
    if b == 1:
        acc[k] = p if fresh else acc[k] + p
        return
    for j in range(ROWS_DEV):
        lo, hi = j * COLS, (j + 1) * COLS
        if b == 0:
            acc[k, lo + reach : hi, :] += p[lo : hi - reach]
        else:
            acc[k, lo : hi - reach, :] += p[lo + reach : hi]


def forward_own(xf, w, acc, base):
    own = xf[pl.ds(base, ROWS_DEV)].reshape(PIX, CIN)
    acc[0] = dot(own, w[0])
    for k in range(1, 4):
        for b in (1, 0, 2):
            add_tap(acc, k, b, dot(own, w[1 + 9 * (k - 1) + 3 + b]), fresh=True)


def forward_others(xf, w, acc, xs, base):
    for k in range(1, 4):
        reach = 12 * k

        @pl.loop(0, 2)
        def _(half, k=k, reach=reach):
            a = 2 * half
            start = base + (a - 1) * reach
            valid = jnp.logical_and(start + ROWS_DEV > 0, start < ROWS)

            @pl.when(valid)
            def _():
                for j in range(ROWS_DEV):
                    r = start + j
                    inside = jnp.logical_and(r >= 0, r < ROWS)
                    row = xf[jnp.clip(r, 0, ROWS - 1)]
                    xs[j * COLS : (j + 1) * COLS, :] = jnp.where(inside, row, jnp.zeros_like(row))
                for b in range(3):
                    add_tap(acc, k, b, dot(xs[...], w[1 + 9 * (k - 1) + 3 * a + b]))


def head(acc, mean, w_pool, lab, wp, wc, cw, d_out, gp_out, gc_out, sp_out):
    pool_pre = dot(jnp.broadcast_to(mean, (16, CIN)), w_pool)[0:1]
    pool_act = jnp.broadcast_to(jax.nn.relu(pool_pre).astype(BF16), (PIX, COUT))
    acts = [jax.nn.relu(acc[k]).astype(BF16) for k in range(4)] + [pool_act]
    y_pre = dot(acts[0], wp[0:COUT])
    for k in range(1, 5):
        y_pre = y_pre + dot(acts[k], wp[k * COUT : (k + 1) * COUT])
    y_act = jax.nn.relu(y_pre).astype(BF16)
    lane = lax.broadcasted_iota(jnp.int32, (PIX, 128), 1)
    lab_t = jnp.concatenate([lab[...].astype(F32), jnp.zeros((8 - ROWS_DEV, COLS), F32)], axis=0)
    lab_t = jnp.concatenate([lab_t, jnp.zeros((8, 128 - COLS), F32)], axis=1).T
    w_cls = jnp.concatenate([wc[...], jnp.zeros((COUT, 125), BF16)], axis=1)
    row = lax.broadcasted_iota(jnp.int32, (1, 128), 1)
    cls_weight = jnp.where(row == 0, cw[0], jnp.where(row == 1, cw[1], jnp.where(row == 2, cw[2], 0.0)))
    label = jnp.concatenate([lab_t[:COLS, j : j + 1] for j in range(ROWS_DEV)], axis=0)
    logits = dot(y_act, w_cls)
    exp_logits = jnp.where(lane < 3, jnp.exp(logits), 0.0)
    prob = exp_logits / jnp.sum(exp_logits, axis=1, keepdims=True)
    onehot = jnp.where(lane.astype(F32) == label, 1.0, 0.0)
    weight = jnp.sum(onehot * cls_weight, axis=1, keepdims=True)
    d_logits = ((prob - onehot) * weight * (loss_scale / FIELD)).astype(BF16)
    d_y = jnp.where(y_pre > 0, dot(d_logits, w_cls, ((1,), (1,))), 0.0).astype(BF16)
    for k in range(4):
        d_cat = dot(d_y, wp[k * COUT : (k + 1) * COUT], ((1,), (1,)))
        d_out[k] = jnp.where(acc[k] > 0, d_cat, 0.0).astype(BF16).reshape(ROWS_DEV, COLS, COUT)
    d_cat = dot(d_y, wp[4 * COUT : 5 * COUT], ((1,), (1,)))
    s_pool = jnp.sum(jnp.where(pool_pre > 0, d_cat, 0.0), axis=0, keepdims=True)
    sp_out[...] = jnp.broadcast_to(s_pool, (8, COUT))
    gc_out[...] = dot(y_act, d_logits, ((0,), (0,))).astype(BF16)

    def rest():
        for k in range(5):
            gp_out[k * COUT : (k + 1) * COUT, :] = dot(acts[k], d_y, ((0,), (0,))).astype(BF16)

    return rest


def branch_of(tap):
    return jnp.where(tap == 0, 0, jnp.minimum((tap - 1) // 9 + 1, 3))


def pick(i, values):
    r = jnp.int32(values[-1])
    for j, v in enumerate(values[:-1]):
        r = jnp.where(i == j, v, r)
    return r


def share_taps(s):
    return (29 * s) // 8, jnp.minimum((29 * s + 28) // 8, TAPS - 1)


def row_blocks(slot):
    table = []
    for s in range(NS):
        lo, hi = (29 * s) // 8, min((29 * s + 28) // 8, TAPS - 1)
        bits = 0
        k0 = 0 if lo == 0 else (lo - 1) // 9 + 1
        for t in range(lo, hi + 1):
            k = 0 if t == 0 else (t - 1) // 9 + 1
            if (k != k0) != (slot == 1):
                continue
            a = 1 if k == 0 else (t - 1) % 9 // 3
            off = (a - 1) * 12 * k
            for h in range(ROWS):
                if 0 <= h + off < ROWS:
                    bits |= 1 << (h // ROWS_DEV)
        table.append(bits)
    return table


def wanted(slot, share, block):
    return lax.rem(lax.shift_right_logical(pick(share, row_blocks(slot)), block), 2) == 1


def d_copies(i, src_block, share, target, bufs, sems):
    d, gp, gc, sp, dbuf, pbuf, cbuf, sbuf = bufs
    ssem, rsem = sems
    lo, hi = share_taps(share)

    def make(j, src, dst):
        return pltpu.make_async_remote_copy(
            src, dst, ssem.at[i, j], rsem.at[i, j], device_id=target, device_id_type=MESH
        )

    return (
        make(0, d.at[branch_of(lo)], dbuf.at[0, block_rows(src_block)]),
        make(1, d.at[branch_of(hi)], dbuf.at[1, block_rows(src_block)]),
        make(2, gp.at[pl.ds(share * PROJ_SHARE, PROJ_SHARE)], pbuf.at[src_block]),
        make(3, gc.at[pl.ds(share * CLS_SHARE, CLS_SHARE)], cbuf.at[src_block]),
        make(4, sp, sbuf.at[src_block]),
    )


def shift_block(slot, block, rows_of, dsh):
    _, z, core, _ = place()
    first, last = share_taps(4 * core + z)
    k0 = branch_of(first)

    @pl.loop(0, 5)
    def _(ti):
        tap = first + ti
        k = branch_of(tap)
        b = jnp.where(k == 0, 1, lax.rem(tap + 2, 3))
        uses = jnp.logical_and(tap <= last, (k != k0) == (slot == 1))

        @pl.when(uses)
        def _():
            for kk in range(1, 4):
                reach = 12 * kk
                for bb in (0, 2):

                    @pl.when(jnp.logical_and(k == kk, b == bb))
                    def _(bb=bb, reach=reach):
                        @pl.loop(0, ROWS_DEV)
                        def _(j):
                            v = rows_of(j).astype(F32)
                            zero = jnp.zeros((reach, COUT), F32)
                            if bb == 0:
                                v = jnp.concatenate([v[reach:], zero], axis=0)
                            else:
                                v = jnp.concatenate([zero, v[: COLS - reach]], axis=0)
                            dsh[ti, block * ROWS_DEV + j] = v.astype(BF16)

            @pl.when(b == 1)
            def _():
                @pl.loop(0, ROWS_DEV)
                def _(j):
                    dsh[ti, block * ROWS_DEV + j] = rows_of(j)


def weight_gradient(xt, dsh, acc, o_ref, plane, first_half):
    _, z, core, _ = place()
    share = 4 * core + z
    first, last = share_taps(share)
    parts = CIN // M_TILE

    @pl.loop(0, 5 * parts)
    def _(step):
        ti, part = step // parts, lax.rem(step, parts)
        tap = first + ti
        row0 = tap * CIN + part * M_TILE - SHARE * share
        touches = jnp.logical_and(row0 > -M_TILE, row0 < SHARE)

        @pl.when(jnp.logical_and(tap <= last, touches))
        def _():
            k = branch_of(tap)
            a = jnp.where(k == 0, 1, lax.rem(tap + 8, 9) // 3)
            off = (a - 1) * 12 * k
            half_rows = ROWS // 2
            lo = jnp.maximum(plane * half_rows, -off)
            hi = jnp.minimum(plane * half_rows + half_rows, ROWS - off)
            n = jnp.maximum(hi - lo, 0)
            m = pl.ds(pl.multiple_of(part * M_TILE, M_TILE), M_TILE)
            if first_half:
                acc[ti, m] = jnp.zeros((M_TILE, COUT), F32)

            def add(row, rows):
                px = pl.ds(pl.multiple_of((row + off) * COLS, 128), rows * COLS)
                dd = dsh[ti, pl.ds(row, rows)].reshape(rows * COLS, COUT)
                acc[ti, m] += dot(xt[m, px], dd)

            def chunk(c, _):
                add(lo + c * 8, 8)
                return 0

            lax.fori_loop(0, n // 8, chunk, 0)

            @pl.when(lax.rem(n, 8) == 4)
            def _():
                add(hi - 4, 4)

            if not first_half:
                for u in range(M_TILE // 128):
                    at = row0 + 128 * u

                    @pl.when(jnp.logical_and(at >= 0, at < SHARE))
                    def _(u=u, at=at):
                        src = pl.ds(pl.multiple_of(part * M_TILE + 128 * u, 128), 128)
                        o_ref[pl.ds(pl.multiple_of(at, 128), 128), :] = acc[ti, src].astype(BF16)


def finish(o_ref, pbuf, cbuf, sbuf, mean_ref, share):
    total = pbuf[0].astype(F32)
    for s in range(1, NS):
        total = total + pbuf[s].astype(F32)
    o_ref[SHARE : SHARE + PROJ_SHARE, :] = total.astype(BF16)
    total = cbuf[0].astype(F32)
    for s in range(1, NS):
        total = total + cbuf[s].astype(F32)
    total = total.astype(BF16)
    o_ref[SHARE + PROJ_SHARE :, :] = jnp.concatenate([total, total], axis=1)

    @pl.when(share == NS - 1)
    def _():
        column = mean_ref[...].T[:, 0:1]
        total = jnp.zeros((CIN, COUT), F32)
        for s in range(NS):
            total = total + (column * sbuf[s, 0:1, :]).astype(BF16).astype(F32)
        o_ref[SHARE - CIN : SHARE, :] = total.astype(BF16)


def kernel(
    x_hbm, lab_ref, w_ref, wp, wc, cw, o_ref,
    xf, w, acc, xs, lab, d, gp, gc, sp, mean_ref, xt, dbuf, pbuf, cbuf, sbuf, dsh, acc_w,
    gs, gr, ds_, dr, lsem, wsem,
):
    xh, z, core, rep0 = place()
    share = 4 * core + z
    base = share * ROWS_DEV
    load = pltpu.make_async_copy(w_ref, w, wsem)
    load.start()
    entry_barrier()

    def while_waiting(xf):
        load.wait()
        forward_own(xf, w, acc, base)

    drain = gather_field(x_hbm, lab_ref, xf, lab, gs, gr, lsem, while_waiting)
    mean = field_mean(xf)
    mean_ref[...] = jnp.broadcast_to(mean.astype(F32), (8, CIN))
    forward_others(xf, w, acc, xs, base)
    rest = head(acc, mean, w[TAPS], lab, wp, wc, cw, d, gp, gc, sp)

    bufs, sems = (d, gp, gc, sp, dbuf, pbuf, cbuf, sbuf), (ds_, dr)
    sent = []
    for i, (dz, late) in enumerate(ORDER):
        z2 = lax.rem(z + dz, 4)
        c2 = jnp.bitwise_xor(core, other_core(dz, late, z2))
        t = 4 * c2 + z2
        c = d_copies(i, share, t, device(xh, z2, c2, rep0), bufs, sems)
        flags = (wanted(0, t, share), wanted(1, t, share))
        sent.append((c, flags, t))
        pl.when(flags[0])(c[0].start)
        pl.when(flags[1])(c[1].start)
    rest()
    transpose_field(xf, xt)
    for c, _, t in sent:
        c[2].start()
        c[3].start()
        pl.when(t == NS - 1)(c[4].start)

    lo, hi = share_taps(share)
    kb0, kb1 = branch_of(lo), branch_of(hi)
    pl.when(wanted(0, share, share))(lambda: shift_block(0, share, lambda j: d[kb0, j], dsh))
    pl.when(wanted(1, share, share))(lambda: shift_block(1, share, lambda j: d[kb1, j], dsh))

    def source(i):
        dz, late = pick(i, [o[0] for o in ORDER]), pick(i, [o[1] for o in ORDER])
        c2 = jnp.bitwise_xor(core, other_core(dz, late, z))
        z2 = lax.rem(z - dz + 4, 4)
        return 4 * c2 + z2, device(xh, z2, c2, rep0)

    def receive(i, _):
        block, dev = source(i)
        c = d_copies(i, block, share, dev, bufs, sems)
        for slot in range(2):

            @pl.when(wanted(slot, share, block))
            def _(slot=slot):
                c[slot].wait_recv()
                shift_block(slot, block, lambda j: dbuf[slot, block * ROWS_DEV + j], dsh)

        return 0

    far = far_first(z)
    lax.fori_loop(0, 3 + far, receive, 0)
    weight_gradient(xt, dsh, acc_w, o_ref, jnp.bitwise_xor(core, far), True)
    lax.fori_loop(3 + far, NS - 1, receive, 0)
    weight_gradient(xt, dsh, acc_w, o_ref, jnp.bitwise_xor(1 - core, far), False)
    pbuf[share] = gp[pl.ds(pl.multiple_of(share * PROJ_SHARE, 32), PROJ_SHARE), :]
    cbuf[share] = gc[pl.ds(pl.multiple_of(share * CLS_SHARE, 32), CLS_SHARE), :]
    sbuf[share] = sp[...]

    @pl.loop(0, NS - 1)
    def _(i):
        block, dev = source(i)
        c = d_copies(i, block, share, dev, bufs, sems)
        c[2].wait_recv()
        c[3].wait_recv()
        pl.when(share == NS - 1)(c[4].wait_recv)

    finish(o_ref, pbuf, cbuf, sbuf, mean_ref, share)
    drain()
    for c, flags, t in sent:
        pl.when(flags[0])(c[0].wait_send)
        pl.when(flags[1])(c[1].wait_send)
        c[2].wait_send()
        c[3].wait_send()
        pl.when(t == NS - 1)(c[4].wait_send)


def average(own, partner, own_tail, partner_tail, avg_in, avg_proj, avg_cls):
    avg_in[...] = (own[...].astype(F32) + partner[...].astype(F32)) * 0.5

    @pl.when(pl.program_id(0) == 0)
    def _():
        mean = (own_tail[...].astype(F32) + partner_tail[...].astype(F32)) * 0.5
        avg_proj[...] = mean[:PROJ_SHARE]
        avg_cls[...] = mean[PROJ_SHARE:, :3]


def home(device_index, mask):
    sp, rep = device_index // 16, device_index % 16
    xh, z, core = sp // 4, sp % 4, rep % 2
    return (4 * core + z) * 16 + ((rep - core + xh) ^ mask)


def per_device(features, labels, w_in, w_proj, w_cls, class_weight, matching):
    x = features[0]
    vmem = pl.BlockSpec(memory_space=pltpu.VMEM)
    hbm = pl.BlockSpec(memory_space=pl.ANY)
    done = pl.pallas_call(
        kernel,
        out_shape=jax.ShapeDtypeStruct((OUT_ROWS, COUT), BF16),
        in_specs=[hbm, vmem, hbm, vmem, vmem, pl.BlockSpec(memory_space=pltpu.SMEM)],
        out_specs=vmem,
        scratch_shapes=[
            pltpu.VMEM((ROWS, COLS, CIN), BF16),
            pltpu.VMEM((29, CIN, COUT), BF16),
            pltpu.VMEM((4, PIX, COUT), F32),
            pltpu.VMEM((PIX, CIN), BF16),
            pltpu.VMEM((ROWS_DEV, COLS), jnp.int32),
            pltpu.VMEM((4, ROWS_DEV, COLS, COUT), BF16),
            pltpu.VMEM((5 * COUT, COUT), BF16),
            pltpu.VMEM((COUT, 128), BF16),
            pltpu.VMEM((8, COUT), F32),
            pltpu.VMEM((8, CIN), F32),
            pltpu.VMEM((CIN, FIELD), BF16),
            pltpu.VMEM((2, ROWS, COLS, COUT), BF16),
            pltpu.VMEM((NS, PROJ_SHARE, COUT), BF16),
            pltpu.VMEM((NS, CLS_SHARE, 128), BF16),
            pltpu.VMEM((NS, 8, COUT), F32),
            pltpu.VMEM((5, ROWS, COLS, COUT), BF16),
            pltpu.VMEM((5, CIN, COUT), F32),
            pltpu.SemaphoreType.DMA((15,)),
            pltpu.SemaphoreType.DMA((15,)),
            pltpu.SemaphoreType.DMA((NS - 1, 5)),
            pltpu.SemaphoreType.DMA((NS - 1, 5)),
            pltpu.SemaphoreType.DMA,
            pltpu.SemaphoreType.DMA,
        ],
        compiler_params=pltpu.CompilerParams(collective_id=0, has_side_effects=True, vmem_limit_bytes=VMEM_LIMIT),
        name="field_gradient",
    )(x, labels[0], w_in, w_proj, w_cls, class_weight)

    def deliver(mask, value):
        n = lax.axis_size("rep") * lax.axis_size("space")
        own = lax.ppermute(value, ("space", "rep"), [(i, home(i, 0)) for i in range(n)])
        partner = lax.ppermute(value, ("space", "rep"), [(i, home(i, mask)) for i in range(n)])
        return own, partner

    own, partner = lax.switch(matching[0] - 1, [functools.partial(deliver, m) for m in range(1, 16)], done)

    steps = 2
    main = pl.BlockSpec((SHARE // steps, COUT), lambda i: (i, 0))
    tail = pl.BlockSpec((pl.Element(OUT_ROWS - SHARE), pl.Element(COUT)), lambda i: (SHARE, 0))
    avg_in, avg_proj, avg_cls = pl.pallas_call(
        average,
        grid=(steps,),
        out_shape=(
            jax.ShapeDtypeStruct((SHARE, COUT), F32),
            jax.ShapeDtypeStruct((PROJ_SHARE, COUT), F32),
            jax.ShapeDtypeStruct((CLS_SHARE, 3), F32),
        ),
        in_specs=[main, main, tail, tail],
        out_specs=(
            main,
            pl.BlockSpec((PROJ_SHARE, COUT), lambda i: (0, 0)),
            pl.BlockSpec((CLS_SHARE, 3), lambda i: (0, 0)),
        ),
        name="average",
    )(own, partner, own, partner)
    return avg_in[None], avg_proj[None], avg_cls[None]


def solution(mesh):
    return jax.shard_map(
        per_device,
        mesh=mesh,
        in_specs=(P("rep", "space", None, None), P("rep", "space", None), P(), P(), P(), P(), P()),
        out_specs=(P("rep", "space", None), P("rep", "space", None), P("rep", "space", None)),
        check_vma=False,
    )
```

```python
import functools

import jax
import jax.numpy as jnp
from jax import lax
from jax.experimental import pallas as pl
from jax.experimental.pallas import tpu as pltpu
from jax.sharding import PartitionSpec as P

MESH = pl.DeviceIdType.MESH
F32 = jnp.float32
BF16 = jnp.bfloat16

NS = 8
ROWS_DEV = 5
ROWS = 40
COLS = 96
CIN = 1024
COUT = 256
PIX = ROWS_DEV * COLS
FIELD = ROWS * COLS
TAPS = 28
SHARE = 29 * CIN // NS
PROJ_SHARE = 5 * COUT // NS
CLS_SHARE = COUT // NS
OUT_ROWS = SHARE + PROJ_SHARE + CLS_SHARE
M_TILE = 1024
VMEM_LIMIT = 62 * 2**20
loss_scale = 1024.0


def dot(a, b, dims=((1,), (0,))):
    return lax.dot_general(a, b, (dims, ((), ())), preferred_element_type=F32)


def place():
    sp, rep = lax.axis_index("space"), lax.axis_index("rep")
    core = lax.rem(rep, 2)
    return sp // 4, lax.rem(sp, 4), core, rep - core


def device(xh, z, core, rep0):
    return {"space": xh * 4 + lax.rem(z + 8, 4), "rep": rep0 + core}


def block_rows(block, first=0, count=ROWS_DEV):
    return pl.ds(block * ROWS_DEV + first, count)


ORDER = ((1, 0), (3, 0), (2, 0), (0, 1), (1, 1), (3, 1), (2, 1))


def far_first(z):
    return jnp.where(jnp.logical_or(z == 0, z == 3), 1, 0)


def other_core(dz, late, z_target):
    return jnp.where(dz == 0, 1, jnp.bitwise_xor(late, far_first(z_target)))


def entry_barrier():
    xh, z, core, rep0 = place()
    barrier = pltpu.get_barrier_semaphore()

    def signal(dev):
        pl.semaphore_signal(barrier, inc=1, device_id=dev, device_id_type=MESH)

    for dz, dc in ((1, 0), (2, 0), (3, 0), (0, 1), (1, 1), (2, 1), (3, 1)):
        signal(device(xh, z + dz, jnp.bitwise_xor(core, dc), rep0))

    @pl.when(xh != core)
    def _():
        signal(device(core, z, xh, rep0))

    pl.semaphore_wait(barrier, 7 + jnp.where(xh != core, 1, 0))


def gather_field(x_hbm, lab_ref, xf, lab, ssem, rsem, lsem, while_waiting, before_last):
    xh, z, core, rep0 = place()
    way = 1 - 2 * core
    mine = 4 * core + z
    sibling = device(xh, z, 1 - core, rep0)

    def blk(zz, plane=core):
        return plane * 4 + lax.rem(zz + 8, 4)

    def message(m, block, first, count, target):
        rows = block_rows(block, first, count)
        return pltpu.make_async_remote_copy(
            xf.at[rows], xf.at[rows], ssem.at[m], rsem.at[m], device_id=target, device_id_type=MESH
        )

    partner = device(core, z, xh, rep0)
    swap = pltpu.make_async_remote_copy(
        x_hbm, xf.at[block_rows(4 * xh + z)], ssem.at[13], rsem.at[13], device_id=partner, device_id_type=MESH
    )
    swap_in = pltpu.make_async_remote_copy(
        x_hbm, xf.at[block_rows(mine)], ssem.at[13], rsem.at[13], device_id=partner, device_id_type=MESH
    )
    swap_lab = pltpu.make_async_remote_copy(
        lab_ref, lab, ssem.at[14], rsem.at[14], device_id=partner, device_id_type=MESH
    )
    local = pltpu.make_async_copy(x_hbm, xf.at[block_rows(mine)], lsem)

    @pl.when(xh != core)
    def _():
        swap.start()
        swap_lab.start()
        swap_in.wait_recv()
        swap_lab.wait_recv()

    @pl.when(xh == core)
    def _():
        local.start()
        lab[...] = lab_ref[...]
        local.wait()

    out = []

    def send(*args):
        c = message(*args)
        c.start()
        out.append(c)

    def arrived(m, block, first, count):
        message(m, block, first, count, sibling).wait_recv()

    ahead, behind = device(xh, z + way, core, rep0), device(xh, z - way, core, rep0)
    send(0, mine, 0, 3, ahead)
    send(1, mine, 3, 2, behind)
    send(2, mine, 3, 2, ahead)
    send(3, mine, 0, 3, behind)
    send(6, mine, 0, 5, sibling)
    while_waiting(xf)
    arrived(0, blk(z - way), 0, 3)
    send(4, blk(z - way), 0, 3, ahead)
    arrived(1, blk(z + way), 3, 2)
    send(5, blk(z + way), 3, 2, behind)
    send(7, blk(z - way), 0, 3, sibling)
    send(8, blk(z + way), 3, 2, sibling)
    arrived(2, blk(z - way), 3, 2)
    send(9, blk(z - way), 3, 2, sibling)
    arrived(3, blk(z + way), 0, 3)
    send(10, blk(z + way), 0, 3, sibling)
    other = 1 - core
    arrived(6, blk(z, other), 0, 5)
    arrived(7, blk(z + way, other), 0, 3)
    arrived(8, blk(z - way, other), 3, 2)
    arrived(9, blk(z + way, other), 3, 2)
    arrived(10, blk(z - way, other), 0, 3)
    before_last([blk(z + i, plane) for i in (0, 1, 3) for plane in (core, other)])
    arrived(5, blk(z + 2), 3, 2)
    send(11, blk(z + 2), 3, 2, sibling)
    arrived(4, blk(z + 2), 0, 3)
    send(12, blk(z + 2), 0, 3, sibling)
    arrived(11, blk(z + 2, other), 3, 2)
    arrived(12, blk(z + 2, other), 0, 3)

    last = [blk(z + 2, core), blk(z + 2, other)]

    def drain():
        for c in out:
            c.wait_send()

        @pl.when(xh != core)
        def _():
            swap.wait_send()
            swap_lab.wait_send()

    return last, drain


def transpose_field(xf, xt):
    @pl.loop(0, ROWS // 4)
    def _(c):
        v = xf[pl.ds(c * 4, 4)].reshape(4 * COLS, CIN)
        xt[:, pl.ds(pl.multiple_of(c * (4 * COLS), 128), 4 * COLS)] = v.T


def add_rows(xf, total, blocks):
    def add(r, total, block):
        v = xf[block * ROWS_DEV + r].astype(F32)
        return total + jnp.sum(v.reshape(COLS // 8, 8, CIN), axis=0)

    for block in blocks:
        total = lax.fori_loop(0, ROWS_DEV, functools.partial(add, block=block), total)
    return total


def add_tap(acc, k, b, p, fresh=False):
    reach = 12 * k
    if b == 1:
        acc[k] = p if fresh else acc[k] + p
        return
    for j in range(ROWS_DEV):
        lo, hi = j * COLS, (j + 1) * COLS
        if b == 0:
            acc[k, lo + reach : hi, :] += p[lo : hi - reach]
        else:
            acc[k, lo : hi - reach, :] += p[lo + reach : hi]


def forward_own(xf, w, acc, base):
    own = xf[pl.ds(base, ROWS_DEV)].reshape(PIX, CIN)
    acc[0] = dot(own, w[0])
    for k in range(1, 4):
        for b in (1, 0, 2):
            add_tap(acc, k, b, dot(own, w[1 + 9 * (k - 1) + 3 + b]), fresh=True)


def forward_others(xf, w, acc, xs, base, rates):
    for k in rates:
        reach = 12 * k

        @pl.loop(0, 2)
        def _(half, k=k, reach=reach):
            a = 2 * half
            start = base + (a - 1) * reach
            valid = jnp.logical_and(start + ROWS_DEV > 0, start < ROWS)

            @pl.when(valid)
            def _():
                for j in range(ROWS_DEV):
                    r = start + j
                    inside = jnp.logical_and(r >= 0, r < ROWS)
                    row = xf[jnp.where(inside, r, base)]
                    xs[j * COLS : (j + 1) * COLS, :] = jnp.where(inside, row, jnp.zeros_like(row))
                for b in range(3):
                    add_tap(acc, k, b, dot(xs[...], w[1 + 9 * (k - 1) + 3 * a + b]))


def head(acc, mean, w_pool, lab, wp, wc, cw, d_out, gp_out, gc_out, sp_out):
    pool_pre = dot(jnp.broadcast_to(mean, (16, CIN)), w_pool)[0:1]
    pool_act = jnp.broadcast_to(jax.nn.relu(pool_pre).astype(BF16), (PIX, COUT))
    acts = [jax.nn.relu(acc[k]).astype(BF16) for k in range(4)] + [pool_act]
    y_pre = dot(acts[0], wp[0:COUT])
    for k in range(1, 5):
        y_pre = y_pre + dot(acts[k], wp[k * COUT : (k + 1) * COUT])
    y_act = jax.nn.relu(y_pre).astype(BF16)
    lane = lax.broadcasted_iota(jnp.int32, (PIX, 128), 1)
    lab_t = jnp.concatenate([lab[j].astype(F32) for j in range(ROWS_DEV)] + [jnp.zeros((8 - ROWS_DEV, COLS), F32)], axis=0)
    lab_t = jnp.concatenate([lab_t, jnp.zeros((8, 128 - COLS), F32)], axis=1).T
    w_cls = jnp.concatenate([wc[...].astype(F32), jnp.zeros((125, COUT), F32)], axis=0).astype(BF16)
    row = lax.broadcasted_iota(jnp.int32, (1, 128), 1)
    cls_weight = jnp.where(row == 0, cw[0], jnp.where(row == 1, cw[1], jnp.where(row == 2, cw[2], 0.0)))
    label = jnp.concatenate([lab_t[:COLS, j : j + 1] for j in range(ROWS_DEV)], axis=0)
    logits = dot(y_act, w_cls, ((1,), (1,)))
    exp_logits = jnp.where(lane < 3, jnp.exp(logits), 0.0)
    prob = exp_logits / jnp.sum(exp_logits, axis=1, keepdims=True)
    onehot = jnp.where(lane.astype(F32) == label, 1.0, 0.0)
    weight = jnp.sum(onehot * cls_weight, axis=1, keepdims=True)
    d_logits = ((prob - onehot) * weight * (loss_scale / FIELD)).astype(BF16)
    d_y = jnp.where(y_pre > 0, dot(d_logits, w_cls), 0.0).astype(BF16)
    for k in range(4):
        d_cat = dot(d_y, wp[k * COUT : (k + 1) * COUT], ((1,), (1,)))
        d_out[k] = jnp.where(acc[k] > 0, d_cat, 0.0).astype(BF16).reshape(ROWS_DEV, COLS, COUT)
    d_cat = dot(d_y, wp[4 * COUT : 5 * COUT], ((1,), (1,)))
    s_pool = jnp.sum(jnp.where(pool_pre > 0, d_cat, 0.0), axis=0, keepdims=True)
    sp_out[...] = jnp.broadcast_to(s_pool, (8, COUT))
    gc_out[...] = dot(y_act, d_logits, ((0,), (0,))).astype(BF16)

    def rest():
        for k in range(5):
            gp_out[k * COUT : (k + 1) * COUT, :] = dot(acts[k], d_y, ((0,), (0,))).astype(BF16)

    return rest


def branch_of(tap):
    return jnp.where(tap == 0, 0, jnp.minimum((tap - 1) // 9 + 1, 3))


def pick(i, values):
    r = jnp.int32(values[-1])
    for j, v in enumerate(values[:-1]):
        r = jnp.where(i == j, v, r)
    return r


def share_taps(s):
    return (29 * s) // 8, jnp.minimum((29 * s + 28) // 8, TAPS - 1)


def row_blocks(slot):
    table = []
    for s in range(NS):
        lo, hi = (29 * s) // 8, min((29 * s + 28) // 8, TAPS - 1)
        bits = 0
        k0 = 0 if lo == 0 else (lo - 1) // 9 + 1
        for t in range(lo, hi + 1):
            k = 0 if t == 0 else (t - 1) // 9 + 1
            if (k != k0) != (slot == 1):
                continue
            a = 1 if k == 0 else (t - 1) % 9 // 3
            off = (a - 1) * 12 * k
            for h in range(ROWS):
                if 0 <= h + off < ROWS:
                    bits |= 1 << (h // ROWS_DEV)
        table.append(bits)
    return table


def wanted(slot, share, block):
    return lax.rem(lax.shift_right_logical(pick(share, row_blocks(slot)), block), 2) == 1


def d_copies(i, src_block, share, target, bufs, sems):
    d, sp, dbuf, sbuf = bufs
    ssem, rsem = sems
    lo, hi = share_taps(share)

    def make(j, src, dst):
        return pltpu.make_async_remote_copy(
            src, dst, ssem.at[i, j], rsem.at[i, j], device_id=target, device_id_type=MESH
        )

    return (
        make(0, d.at[branch_of(lo)], dbuf.at[0, block_rows(src_block)]),
        make(1, d.at[branch_of(hi)], dbuf.at[1, block_rows(src_block)]),
        make(2, sp, sbuf.at[src_block]),
    )


def shift_block(slot, block, rows_of, dsh):
    _, z, core, _ = place()
    first, last = share_taps(4 * core + z)
    k0 = branch_of(first)

    @pl.loop(0, 5)
    def _(ti):
        tap = first + ti
        k = branch_of(tap)
        b = jnp.where(k == 0, 1, lax.rem(tap + 2, 3))
        uses = jnp.logical_and(tap <= last, (k != k0) == (slot == 1))

        @pl.when(uses)
        def _():
            for kk in range(1, 4):
                reach = 12 * kk
                for bb in (0, 2):

                    @pl.when(jnp.logical_and(k == kk, b == bb))
                    def _(bb=bb, reach=reach):
                        @pl.loop(0, ROWS_DEV)
                        def _(j):
                            v = rows_of(j).astype(F32)
                            zero = jnp.zeros((reach, COUT), F32)
                            if bb == 0:
                                v = jnp.concatenate([v[reach:], zero], axis=0)
                            else:
                                v = jnp.concatenate([zero, v[: COLS - reach]], axis=0)
                            dsh[ti, block * ROWS_DEV + j] = v.astype(BF16)

            @pl.when(b == 1)
            def _():
                @pl.loop(0, ROWS_DEV)
                def _(j):
                    dsh[ti, block * ROWS_DEV + j] = rows_of(j)


def weight_gradient(xt, dsh, acc, o_ref, plane, first_half):
    _, z, core, _ = place()
    share = 4 * core + z
    first, last = share_taps(share)
    parts = CIN // M_TILE

    @pl.loop(0, 5 * parts)
    def _(step):
        ti, part = step // parts, lax.rem(step, parts)
        tap = first + ti
        row0 = tap * CIN + part * M_TILE - SHARE * share
        touches = jnp.logical_and(row0 > -M_TILE, row0 < SHARE)

        @pl.when(jnp.logical_and(tap <= last, touches))
        def _():
            k = branch_of(tap)
            a = jnp.where(k == 0, 1, lax.rem(tap + 8, 9) // 3)
            off = (a - 1) * 12 * k
            half_rows = ROWS // 2
            lo = jnp.maximum(plane * half_rows, -off)
            hi = jnp.minimum(plane * half_rows + half_rows, ROWS - off)
            n = jnp.maximum(hi - lo, 0)
            m = pl.ds(pl.multiple_of(part * M_TILE, M_TILE), M_TILE)
            if first_half:
                acc[ti, m] = jnp.zeros((M_TILE, COUT), F32)

            def add(row, rows):
                px = pl.ds(pl.multiple_of((row + off) * COLS, 128), rows * COLS)
                dd = dsh[ti, pl.ds(row, rows)].reshape(rows * COLS, COUT)
                acc[ti, m] += dot(xt[m, px], dd)

            def chunk(c, _):
                add(lo + c * 8, 8)
                return 0

            lax.fori_loop(0, n // 8, chunk, 0)

            @pl.when(lax.rem(n, 8) == 4)
            def _():
                add(hi - 4, 4)

            if not first_half:
                for u in range(M_TILE // 128):
                    at = row0 + 128 * u

                    @pl.when(jnp.logical_and(at >= 0, at < SHARE))
                    def _(u=u, at=at):
                        src = pl.ds(pl.multiple_of(part * M_TILE + 128 * u, 128), 128)
                        o_ref[pl.ds(pl.multiple_of(at, 128), 128), :] = acc[ti, src].astype(BF16)


def finish(o_ref, pbuf, cbuf, sbuf, mean_ref, share):
    total = pbuf[0].astype(F32)
    for s in range(1, 4):
        total = total + pbuf[s].astype(F32)
    o_ref[SHARE : SHARE + PROJ_SHARE, :] = total.astype(BF16)
    total = cbuf[0].astype(F32)
    for s in range(1, 4):
        total = total + cbuf[s].astype(F32)
    total = total.astype(BF16)
    o_ref[SHARE + PROJ_SHARE :, :] = jnp.concatenate([total, total], axis=1)

    @pl.when(share == NS - 1)
    def _():
        column = mean_ref[...].T[:, 0:1]
        total = jnp.zeros((CIN, COUT), F32)
        for s in range(NS):
            total = total + (column * sbuf[s, 0:1, :]).astype(BF16).astype(F32)
        o_ref[SHARE - CIN : SHARE, :] = total.astype(BF16)


def kernel(
    x_hbm, lab_ref, w_ref, wp, wc, cw, o_ref,
    xf, w, acc, xs, lab, d, gp, gc, sp, mean_ref, xt, dbuf, gp_in, gc_in, gp_sum, gc_sum, pbuf, cbuf, sbuf, dsh, acc_w,
    gs, gr, ds_, dr, ps, pr, lsem, wsem,
):
    xh, z, core, rep0 = place()
    share = 4 * core + z
    base = share * ROWS_DEV
    load = pltpu.make_async_copy(w_ref, w, wsem)
    load.start()
    entry_barrier()

    def while_waiting(xf):
        load.wait()
        forward_own(xf, w, acc, base)

    def before_last(blocks):
        mean_ref[...] = add_rows(xf, jnp.zeros((8, CIN), F32), blocks)
        forward_others(xf, w, acc, xs, base, (2, 3))

    last_blocks, drain = gather_field(x_hbm, lab_ref, xf, lab, gs, gr, lsem, while_waiting, before_last)
    total = add_rows(xf, mean_ref[...], last_blocks)
    mean = (jnp.sum(total, axis=0, keepdims=True) / FIELD).astype(BF16)
    mean_ref[...] = jnp.broadcast_to(mean.astype(F32), (8, CIN))
    forward_others(xf, w, acc, xs, base, (1,))
    rest = head(acc, mean, w[TAPS], lab, wp, wc, cw, d, gp, gc, sp)

    bufs, sems = (d, sp, dbuf, sbuf), (ds_, dr)
    sent = []
    for i, (dz, late) in enumerate(ORDER):
        z2 = lax.rem(z + dz, 4)
        c2 = jnp.bitwise_xor(core, other_core(dz, late, z2))
        t = 4 * c2 + z2
        c = d_copies(i, share, t, device(xh, z2, c2, rep0), bufs, sems)
        flags = (wanted(0, t, share), wanted(1, t, share))
        sent.append((c, flags, t))
        pl.when(flags[0])(c[0].start)
        pl.when(flags[1])(c[1].start)
    rest()
    transpose_field(xf, xt)
    for c, _, t in sent:
        pl.when(t == NS - 1)(c[2].start)
    sibling = device(xh, z, 1 - core, rep0)

    def half(rows, plane):
        return pl.ds(pl.multiple_of(plane * rows, rows), rows)

    def proj_copy(j, from_ref, to_ref, target):
        return pltpu.make_async_remote_copy(
            from_ref, to_ref, ps.at[j], pr.at[j], device_id=target, device_id_type=MESH
        )

    to_sibling = (
        proj_copy(0, gp.at[half(4 * PROJ_SHARE, 1 - core)], gp_in, sibling),
        proj_copy(1, gc.at[half(4 * CLS_SHARE, 1 - core)], gc_in, sibling),
    )
    for c in to_sibling:
        c.start()

    lo, hi = share_taps(share)
    kb0, kb1 = branch_of(lo), branch_of(hi)
    pl.when(wanted(0, share, share))(lambda: shift_block(0, share, lambda j: d[kb0, j], dsh))
    pl.when(wanted(1, share, share))(lambda: shift_block(1, share, lambda j: d[kb1, j], dsh))

    def source(i):
        dz, late = pick(i, [o[0] for o in ORDER]), pick(i, [o[1] for o in ORDER])
        c2 = jnp.bitwise_xor(core, other_core(dz, late, z))
        z2 = lax.rem(z - dz + 4, 4)
        return 4 * c2 + z2, device(xh, z2, c2, rep0)

    def receive(i, _):
        block, dev = source(i)
        c = d_copies(i, block, share, dev, bufs, sems)
        for slot in range(2):

            @pl.when(wanted(slot, share, block))
            def _(slot=slot):
                c[slot].wait_recv()
                shift_block(slot, block, lambda j: dbuf[slot, block * ROWS_DEV + j], dsh)

        return 0

    for c in to_sibling:
        c.wait_recv()
    gp_sum[...] = (gp[half(4 * PROJ_SHARE, core), :].astype(F32) + gp_in[...].astype(F32)).astype(BF16)
    gc_sum[...] = (gc[half(4 * CLS_SHARE, core), :].astype(F32) + gc_in[...].astype(F32)).astype(BF16)
    far = far_first(z)
    lax.fori_loop(0, 3 + far, receive, 0)
    along_z = []
    for i, dz in enumerate((1, 3, 2)):
        z2 = lax.rem(z + dz, 4)
        target = device(xh, z2, core, rep0)
        along_z.append(proj_copy(2 + i, gp_sum.at[pl.ds(z2 * PROJ_SHARE, PROJ_SHARE)], pbuf.at[z], target))
        along_z.append(proj_copy(5 + i, gc_sum.at[pl.ds(z2 * CLS_SHARE, CLS_SHARE)], cbuf.at[z], target))
    for c in along_z:
        c.start()
    weight_gradient(xt, dsh, acc_w, o_ref, jnp.bitwise_xor(core, far), True)
    lax.fori_loop(3 + far, NS - 1, receive, 0)
    weight_gradient(xt, dsh, acc_w, o_ref, jnp.bitwise_xor(1 - core, far), False)
    pbuf[z] = gp_sum[pl.ds(pl.multiple_of(z * PROJ_SHARE, 32), PROJ_SHARE), :]
    cbuf[z] = gc_sum[pl.ds(pl.multiple_of(z * CLS_SHARE, 32), CLS_SHARE), :]
    sbuf[share] = sp[...]
    for i, dz in enumerate((1, 3, 2)):
        z2 = lax.rem(z - dz + 4, 4)
        proj_copy(2 + i, gp_sum.at[pl.ds(0, PROJ_SHARE)], pbuf.at[z2], sibling).wait_recv()
        proj_copy(5 + i, gc_sum.at[pl.ds(0, CLS_SHARE)], cbuf.at[z2], sibling).wait_recv()

    @pl.when(share == NS - 1)
    def _():
        @pl.loop(0, NS - 1)
        def _(i):
            block, dev = source(i)
            d_copies(i, block, share, dev, bufs, sems)[2].wait_recv()

    finish(o_ref, pbuf, cbuf, sbuf, mean_ref, share)
    drain()
    for c, flags, t in sent:
        pl.when(flags[0])(c[0].wait_send)
        pl.when(flags[1])(c[1].wait_send)
        pl.when(t == NS - 1)(c[2].wait_send)
    for c in to_sibling + tuple(along_z):
        c.wait_send()


def average(own, partner, own_tail, partner_tail, avg_in, avg_proj, avg_cls):
    avg_in[...] = (own[...].astype(F32) + partner[...].astype(F32)) * 0.5

    @pl.when(pl.program_id(0) == 0)
    def _():
        mean = (own_tail[...].astype(F32) + partner_tail[...].astype(F32)) * 0.5
        avg_proj[...] = mean[:PROJ_SHARE]
        by_class = mean[PROJ_SHARE:, :128].T
        for c in range(3):
            avg_cls[c] = by_class[c : c + 1, :]


def home(device_index, mask):
    sp, rep = device_index // 16, device_index % 16
    xh, z, core = sp // 4, sp % 4, rep % 2
    return (4 * core + z) * 16 + ((rep - core + xh) ^ mask)


def per_device(features, labels, w_in, w_proj, w_cls, class_weight, matching):
    x = features[0]
    vmem = pl.BlockSpec(memory_space=pltpu.VMEM)
    hbm = pl.BlockSpec(memory_space=pl.ANY)
    done = pl.pallas_call(
        kernel,
        out_shape=jax.ShapeDtypeStruct((OUT_ROWS, COUT), BF16),
        in_specs=[hbm, vmem, hbm, vmem, vmem, pl.BlockSpec(memory_space=pltpu.SMEM)],
        out_specs=vmem,
        scratch_shapes=[
            pltpu.VMEM((ROWS, COLS, CIN), BF16),
            pltpu.VMEM((29, CIN, COUT), BF16),
            pltpu.VMEM((4, PIX, COUT), F32),
            pltpu.VMEM((PIX, CIN), BF16),
            pltpu.VMEM((ROWS_DEV, 1, COLS), jnp.int32),
            pltpu.VMEM((4, ROWS_DEV, COLS, COUT), BF16),
            pltpu.VMEM((5 * COUT, COUT), BF16),
            pltpu.VMEM((COUT, 128), BF16),
            pltpu.VMEM((8, COUT), F32),
            pltpu.VMEM((8, CIN), F32),
            pltpu.VMEM((CIN, FIELD), BF16),
            pltpu.VMEM((2, ROWS, COLS, COUT), BF16),
            pltpu.VMEM((4 * PROJ_SHARE, COUT), BF16),
            pltpu.VMEM((4 * CLS_SHARE, 128), BF16),
            pltpu.VMEM((4 * PROJ_SHARE, COUT), BF16),
            pltpu.VMEM((4 * CLS_SHARE, 128), BF16),
            pltpu.VMEM((4, PROJ_SHARE, COUT), BF16),
            pltpu.VMEM((4, CLS_SHARE, 128), BF16),
            pltpu.VMEM((NS, 8, COUT), F32),
            pltpu.VMEM((5, ROWS, COLS, COUT), BF16),
            pltpu.VMEM((5, CIN, COUT), F32),
            pltpu.SemaphoreType.DMA((15,)),
            pltpu.SemaphoreType.DMA((15,)),
            pltpu.SemaphoreType.DMA((NS - 1, 3)),
            pltpu.SemaphoreType.DMA((NS - 1, 3)),
            pltpu.SemaphoreType.DMA((8,)),
            pltpu.SemaphoreType.DMA((8,)),
            pltpu.SemaphoreType.DMA,
            pltpu.SemaphoreType.DMA,
        ],
        compiler_params=pltpu.CompilerParams(collective_id=0, has_side_effects=True, vmem_limit_bytes=VMEM_LIMIT),
        name="field_gradient",
    )(x, labels.transpose(1, 0, 2), w_in, w_proj, w_cls.T, class_weight)

    def deliver(mask, value):
        n = lax.axis_size("rep") * lax.axis_size("space")
        own = lax.ppermute(value, ("space", "rep"), [(i, home(i, 0)) for i in range(n)])
        partner = lax.ppermute(value, ("space", "rep"), [(i, home(i, mask)) for i in range(n)])
        return own, partner

    own, partner = lax.switch(matching[0] - 1, [functools.partial(deliver, m) for m in range(1, 16)], done)

    steps = 2
    main = pl.BlockSpec((SHARE // steps, COUT), lambda i: (i, 0))
    tail = pl.BlockSpec((pl.Element(OUT_ROWS - SHARE), pl.Element(COUT)), lambda i: (SHARE, 0))
    avg_in, avg_proj, avg_cls = pl.pallas_call(
        average,
        grid=(steps,),
        out_shape=(
            jax.ShapeDtypeStruct((SHARE, COUT), F32),
            jax.ShapeDtypeStruct((PROJ_SHARE, COUT), F32),
            jax.ShapeDtypeStruct((3, 1, CLS_SHARE), F32),
        ),
        in_specs=[main, main, tail, tail],
        out_specs=(
            main,
            pl.BlockSpec((PROJ_SHARE, COUT), lambda i: (0, 0)),
            pl.BlockSpec((3, 1, CLS_SHARE), lambda i: (0, 0, 0)),
        ),
        name="average",
    )(own, partner, own, partner)
    return avg_in[None], avg_proj[None], avg_cls.transpose(1, 2, 0)


def solution(mesh):
    return jax.shard_map(
        per_device,
        mesh=mesh,
        in_specs=(P("rep", "space", None, None), P("rep", "space", None), P(), P(), P(), P(), P()),
        out_specs=(P("rep", "space", None), P("rep", "space", None), P("rep", "space", None)),
        check_vma=False,
    )
```

```python
import functools

import jax
import jax.numpy as jnp
from jax import lax
from jax.experimental import pallas as pl
from jax.experimental.pallas import tpu as pltpu
from jax.sharding import PartitionSpec as P

MESH = pl.DeviceIdType.MESH
F32 = jnp.float32
BF16 = jnp.bfloat16

NS = 8
ROWS_DEV = 5
ROWS = 40
COLS = 96
CIN = 1024
COUT = 256
PIX = ROWS_DEV * COLS
FIELD = ROWS * COLS
TAPS = 28
SHARE = 29 * CIN // NS
PROJ_SHARE = 5 * COUT // NS
CLS_SHARE = COUT // NS
OUT_ROWS = SHARE + PROJ_SHARE + CLS_SHARE
M_TILE = 1024
VMEM_LIMIT = 62 * 2**20
loss_scale = 1024.0


def dot(a, b, dims=((1,), (0,))):
    return lax.dot_general(a, b, (dims, ((), ())), preferred_element_type=F32)


def place():
    sp, rep = lax.axis_index("space"), lax.axis_index("rep")
    core = lax.rem(rep, 2)
    return sp // 4, lax.rem(sp, 4), core, rep - core


def device(xh, z, core, rep0):
    return {"space": xh * 4 + lax.rem(z + 8, 4), "rep": rep0 + core}


def block_rows(block, first=0, count=ROWS_DEV):
    return pl.ds(block * ROWS_DEV + first, count)


ORDER = ((1, 0), (3, 0), (2, 0), (0, 1), (1, 1), (3, 1), (2, 1))


def far_first(z):
    return jnp.where(jnp.logical_or(z == 0, z == 3), 1, 0)


def other_core(dz, late, z_target):
    return jnp.where(dz == 0, 1, jnp.bitwise_xor(late, far_first(z_target)))


def entry_barrier():
    xh, z, core, rep0 = place()
    barrier = pltpu.get_barrier_semaphore()

    def signal(dev):
        pl.semaphore_signal(barrier, inc=1, device_id=dev, device_id_type=MESH)

    for dz, dc in ((1, 0), (2, 0), (3, 0), (0, 1), (1, 1), (2, 1), (3, 1)):
        signal(device(xh, z + dz, jnp.bitwise_xor(core, dc), rep0))

    @pl.when(xh != core)
    def _():
        signal(device(core, z, xh, rep0))

    pl.semaphore_wait(barrier, 7 + jnp.where(xh != core, 1, 0))


def gather_field(x_hbm, lab_ref, xf, lab, ssem, rsem, lsem, while_waiting, before_last):
    xh, z, core, rep0 = place()
    way = 1 - 2 * core
    mine = 4 * core + z
    sibling = device(xh, z, 1 - core, rep0)

    def blk(zz, plane=core):
        return plane * 4 + lax.rem(zz + 8, 4)

    def message(m, block, first, count, target):
        rows = block_rows(block, first, count)
        return pltpu.make_async_remote_copy(
            xf.at[rows], xf.at[rows], ssem.at[m], rsem.at[m], device_id=target, device_id_type=MESH
        )

    partner = device(core, z, xh, rep0)
    swap = pltpu.make_async_remote_copy(
        x_hbm, xf.at[block_rows(4 * xh + z)], ssem.at[13], rsem.at[13], device_id=partner, device_id_type=MESH
    )
    swap_in = pltpu.make_async_remote_copy(
        x_hbm, xf.at[block_rows(mine)], ssem.at[13], rsem.at[13], device_id=partner, device_id_type=MESH
    )
    swap_lab = pltpu.make_async_remote_copy(
        lab_ref, lab, ssem.at[14], rsem.at[14], device_id=partner, device_id_type=MESH
    )
    local = pltpu.make_async_copy(x_hbm, xf.at[block_rows(mine)], lsem)

    @pl.when(xh != core)
    def _():
        swap.start()
        swap_lab.start()
        swap_in.wait_recv()
        swap_lab.wait_recv()

    @pl.when(xh == core)
    def _():
        local.start()
        lab[...] = lab_ref[...]
        local.wait()

    out = []

    def send(*args):
        c = message(*args)
        c.start()
        out.append(c)

    def arrived(m, block, first, count):
        message(m, block, first, count, sibling).wait_recv()

    ahead, behind = device(xh, z + way, core, rep0), device(xh, z - way, core, rep0)
    send(0, mine, 0, 3, ahead)
    send(1, mine, 3, 2, behind)
    send(2, mine, 3, 2, ahead)
    send(3, mine, 0, 3, behind)
    send(6, mine, 0, 5, sibling)
    while_waiting(xf)
    arrived(0, blk(z - way), 0, 3)
    send(4, blk(z - way), 0, 3, ahead)
    arrived(1, blk(z + way), 3, 2)
    send(5, blk(z + way), 3, 2, behind)
    send(7, blk(z - way), 0, 3, sibling)
    send(8, blk(z + way), 3, 2, sibling)
    arrived(2, blk(z - way), 3, 2)
    send(9, blk(z - way), 3, 2, sibling)
    arrived(3, blk(z + way), 0, 3)
    send(10, blk(z + way), 0, 3, sibling)
    other = 1 - core
    arrived(6, blk(z, other), 0, 5)
    arrived(7, blk(z + way, other), 0, 3)
    arrived(8, blk(z - way, other), 3, 2)
    arrived(9, blk(z + way, other), 3, 2)
    arrived(10, blk(z - way, other), 0, 3)
    before_last([blk(z + i, plane) for i in (0, 1, 3) for plane in (core, other)])
    arrived(5, blk(z + 2), 3, 2)
    send(11, blk(z + 2), 3, 2, sibling)
    arrived(4, blk(z + 2), 0, 3)
    send(12, blk(z + 2), 0, 3, sibling)
    arrived(11, blk(z + 2, other), 3, 2)
    arrived(12, blk(z + 2, other), 0, 3)

    last = [blk(z + 2, core), blk(z + 2, other)]

    def drain():
        for c in out:
            c.wait_send()

        @pl.when(xh != core)
        def _():
            swap.wait_send()
            swap_lab.wait_send()

    return last, drain


def transpose_field(xf, xt):
    @pl.loop(0, ROWS // 4)
    def _(c):
        v = xf[pl.ds(c * 4, 4)].reshape(4 * COLS, CIN)
        xt[:, pl.ds(pl.multiple_of(c * (4 * COLS), 128), 4 * COLS)] = v.T


def add_rows(xf, total, blocks):
    def add(r, total, block):
        v = xf[block * ROWS_DEV + r].astype(F32)
        return total + jnp.sum(v.reshape(COLS // 8, 8, CIN), axis=0)

    for block in blocks:
        total = lax.fori_loop(0, ROWS_DEV, functools.partial(add, block=block), total)
    return total


def add_tap(acc, k, b, p, fresh=False):
    reach = 12 * k
    if b == 1:
        acc[k] = p if fresh else acc[k] + p
        return
    for j in range(ROWS_DEV):
        lo, hi = j * COLS, (j + 1) * COLS
        if b == 0:
            acc[k, lo + reach : hi, :] += p[lo : hi - reach]
        else:
            acc[k, lo : hi - reach, :] += p[lo + reach : hi]


def forward_own(xf, w, acc, base):
    own = xf[pl.ds(base, ROWS_DEV)].reshape(PIX, CIN)
    acc[0] = dot(own, w[0])
    for k in range(1, 4):
        for b in (1, 0, 2):
            add_tap(acc, k, b, dot(own, w[1 + 9 * (k - 1) + 3 + b]), fresh=True)


def forward_others(xf, w, acc, xs, base, rates):
    for k in rates:
        reach = 12 * k

        @pl.loop(0, 2)
        def _(half, k=k, reach=reach):
            a = 2 * half
            start = base + (a - 1) * reach
            valid = jnp.logical_and(start + ROWS_DEV > 0, start < ROWS)

            @pl.when(valid)
            def _():
                for j in range(ROWS_DEV):
                    r = start + j
                    inside = jnp.logical_and(r >= 0, r < ROWS)
                    row = xf[jnp.where(inside, r, base)]
                    xs[j * COLS : (j + 1) * COLS, :] = jnp.where(inside, row, jnp.zeros_like(row))
                for b in range(3):
                    add_tap(acc, k, b, dot(xs[...], w[1 + 9 * (k - 1) + 3 * a + b]))


def head(acc, mean, w_pool, lab, wp, wc, cw, d_out, gp_out, gc_out, sp_out):
    pool_pre = dot(jnp.broadcast_to(mean, (16, CIN)), w_pool)[0:1]
    pool_act = jnp.broadcast_to(jax.nn.relu(pool_pre).astype(BF16), (PIX, COUT))
    acts = [jax.nn.relu(acc[k]).astype(BF16) for k in range(4)] + [pool_act]
    y_pre = dot(acts[0], wp[0:COUT])
    for k in range(1, 5):
        y_pre = y_pre + dot(acts[k], wp[k * COUT : (k + 1) * COUT])
    y_act = jax.nn.relu(y_pre).astype(BF16)
    lane = lax.broadcasted_iota(jnp.int32, (PIX, 128), 1)
    lab_t = jnp.concatenate([lab[j].astype(F32) for j in range(ROWS_DEV)] + [jnp.zeros((8 - ROWS_DEV, COLS), F32)], axis=0)
    lab_t = jnp.concatenate([lab_t, jnp.zeros((8, 128 - COLS), F32)], axis=1).T
    w_cls = jnp.concatenate([wc[...].astype(F32), jnp.zeros((125, COUT), F32)], axis=0).astype(BF16)
    row = lax.broadcasted_iota(jnp.int32, (1, 128), 1)
    cls_weight = jnp.where(row == 0, cw[0], jnp.where(row == 1, cw[1], jnp.where(row == 2, cw[2], 0.0)))
    label = jnp.concatenate([lab_t[:COLS, j : j + 1] for j in range(ROWS_DEV)], axis=0)
    logits = dot(y_act, w_cls, ((1,), (1,)))
    exp_logits = jnp.where(lane < 3, jnp.exp(logits), 0.0)
    prob = exp_logits / jnp.sum(exp_logits, axis=1, keepdims=True)
    onehot = jnp.where(lane.astype(F32) == label, 1.0, 0.0)
    weight = jnp.sum(onehot * cls_weight, axis=1, keepdims=True)
    d_logits = ((prob - onehot) * weight * (loss_scale / FIELD)).astype(BF16)
    d_y = jnp.where(y_pre > 0, dot(d_logits, w_cls), 0.0).astype(BF16)
    for k in range(4):
        d_cat = dot(d_y, wp[k * COUT : (k + 1) * COUT], ((1,), (1,)))
        d_out[k] = jnp.where(acc[k] > 0, d_cat, 0.0).astype(BF16).reshape(ROWS_DEV, COLS, COUT)
    d_cat = dot(d_y, wp[4 * COUT : 5 * COUT], ((1,), (1,)))
    s_pool = jnp.sum(jnp.where(pool_pre > 0, d_cat, 0.0), axis=0, keepdims=True)
    sp_out[...] = jnp.broadcast_to(s_pool, (8, COUT))
    gc_out[...] = dot(y_act, d_logits, ((0,), (0,))).astype(BF16)

    def rest():
        for k in range(5):
            gp_out[k * COUT : (k + 1) * COUT, :] = dot(acts[k], d_y, ((0,), (0,))).astype(BF16)

    return rest


def branch_of(tap):
    return jnp.where(tap == 0, 0, jnp.minimum((tap - 1) // 9 + 1, 3))


def pick(i, values):
    r = jnp.int32(values[-1])
    for j, v in enumerate(values[:-1]):
        r = jnp.where(i == j, v, r)
    return r


def share_taps(s):
    return (29 * s) // 8, jnp.minimum((29 * s + 28) // 8, TAPS - 1)


def row_blocks(slot):
    table = []
    for s in range(NS):
        lo, hi = (29 * s) // 8, min((29 * s + 28) // 8, TAPS - 1)
        bits = 0
        k0 = 0 if lo == 0 else (lo - 1) // 9 + 1
        for t in range(lo, hi + 1):
            k = 0 if t == 0 else (t - 1) // 9 + 1
            if (k != k0) != (slot == 1):
                continue
            a = 1 if k == 0 else (t - 1) % 9 // 3
            off = (a - 1) * 12 * k
            for h in range(ROWS):
                if 0 <= h + off < ROWS:
                    bits |= 1 << (h // ROWS_DEV)
        table.append(bits)
    return table


def wanted(slot, share, block):
    return lax.rem(lax.shift_right_logical(pick(share, row_blocks(slot)), block), 2) == 1


def d_copies(i, src_block, share, target, bufs, sems):
    d, sp, dbuf, sbuf = bufs
    ssem, rsem = sems
    lo, hi = share_taps(share)

    def make(j, src, dst):
        return pltpu.make_async_remote_copy(
            src, dst, ssem.at[i, j], rsem.at[i, j], device_id=target, device_id_type=MESH
        )

    return (
        make(0, d.at[branch_of(lo)], dbuf.at[0, block_rows(src_block)]),
        make(1, d.at[branch_of(hi)], dbuf.at[1, block_rows(src_block)]),
        make(2, sp, sbuf.at[src_block]),
    )


def shift_block(slot, block, rows_of, dsh):
    _, z, core, _ = place()
    first, last = share_taps(4 * core + z)
    k0 = branch_of(first)

    @pl.loop(0, 5)
    def _(ti):
        tap = first + ti
        k = branch_of(tap)
        b = jnp.where(k == 0, 1, lax.rem(tap + 2, 3))
        uses = jnp.logical_and(tap <= last, (k != k0) == (slot == 1))

        @pl.when(uses)
        def _():
            for kk in range(1, 4):
                reach = 12 * kk
                for bb in (0, 2):

                    @pl.when(jnp.logical_and(k == kk, b == bb))
                    def _(bb=bb, reach=reach):
                        @pl.loop(0, ROWS_DEV)
                        def _(j):
                            v = rows_of(j).astype(F32)
                            zero = jnp.zeros((reach, COUT), F32)
                            if bb == 0:
                                v = jnp.concatenate([v[reach:], zero], axis=0)
                            else:
                                v = jnp.concatenate([zero, v[: COLS - reach]], axis=0)
                            dsh[ti, block * ROWS_DEV + j] = v.astype(BF16)

            @pl.when(b == 1)
            def _():
                @pl.loop(0, ROWS_DEV)
                def _(j):
                    dsh[ti, block * ROWS_DEV + j] = rows_of(j)


def weight_gradient(xt, dsh, acc, o_ref, plane, first_half):
    _, z, core, _ = place()
    share = 4 * core + z
    first, last = share_taps(share)
    parts = CIN // M_TILE

    @pl.loop(0, 5 * parts)
    def _(step):
        ti, part = step // parts, lax.rem(step, parts)
        tap = first + ti
        row0 = tap * CIN + part * M_TILE - SHARE * share
        touches = jnp.logical_and(row0 > -M_TILE, row0 < SHARE)

        @pl.when(jnp.logical_and(tap <= last, touches))
        def _():
            k = branch_of(tap)
            a = jnp.where(k == 0, 1, lax.rem(tap + 8, 9) // 3)
            off = (a - 1) * 12 * k
            half_rows = ROWS // 2
            lo = jnp.maximum(plane * half_rows, -off)
            hi = jnp.minimum(plane * half_rows + half_rows, ROWS - off)
            n = jnp.maximum(hi - lo, 0)
            m = pl.ds(pl.multiple_of(part * M_TILE, M_TILE), M_TILE)
            if first_half:
                acc[ti, m] = jnp.zeros((M_TILE, COUT), F32)

            def add(row, rows):
                px = pl.ds(pl.multiple_of((row + off) * COLS, 128), rows * COLS)
                dd = dsh[ti, pl.ds(row, rows)].reshape(rows * COLS, COUT)
                acc[ti, m] += dot(xt[m, px], dd)

            def chunk(c, _):
                add(lo + c * 8, 8)
                return 0

            lax.fori_loop(0, n // 8, chunk, 0)

            @pl.when(lax.rem(n, 8) == 4)
            def _():
                add(hi - 4, 4)

            if not first_half:
                for u in range(M_TILE // 128):
                    at = row0 + 128 * u

                    @pl.when(jnp.logical_and(at >= 0, at < SHARE))
                    def _(u=u, at=at):
                        src = pl.ds(pl.multiple_of(part * M_TILE + 128 * u, 128), 128)
                        o_ref[pl.ds(pl.multiple_of(at, 128), 128), :] = acc[ti, src].astype(BF16)


def finish(o_ref, pbuf, cbuf, sbuf, mean_ref, share):
    total = pbuf[0].astype(F32)
    for s in range(1, 4):
        total = total + pbuf[s].astype(F32)
    o_ref[SHARE : SHARE + PROJ_SHARE, :] = total.astype(BF16)
    total = cbuf[0].astype(F32)
    for s in range(1, 4):
        total = total + cbuf[s].astype(F32)
    total = total.astype(BF16)
    o_ref[SHARE + PROJ_SHARE :, :] = jnp.concatenate([total, total], axis=1)

    @pl.when(share == NS - 1)
    def _():
        column = mean_ref[...].T[:, 0:1]
        total = jnp.zeros((CIN, COUT), F32)
        for s in range(NS):
            total = total + (column * sbuf[s, 0:1, :]).astype(BF16).astype(F32)
        o_ref[SHARE - CIN : SHARE, :] = total.astype(BF16)


def kernel(
    x_hbm, lab_ref, w_ref, wp, wc, cw, o_ref,
    xf, w, acc, xs, lab, d, gp, gc, sp, mean_ref, xt, dbuf, gp_in, gc_in, gp_sum, gc_sum, pbuf, cbuf, sbuf, dsh, acc_w,
    gs, gr, ds_, dr, ps, pr, lsem, wsem,
):
    xh, z, core, rep0 = place()
    share = 4 * core + z
    base = share * ROWS_DEV
    load = pltpu.make_async_copy(w_ref, w, wsem)
    load.start()
    entry_barrier()

    def while_waiting(xf):
        load.wait()
        forward_own(xf, w, acc, base)

    def before_last(blocks):
        mean_ref[...] = add_rows(xf, jnp.zeros((8, CIN), F32), blocks)
        forward_others(xf, w, acc, xs, base, (2, 3))

    last_blocks, drain = gather_field(x_hbm, lab_ref, xf, lab, gs, gr, lsem, while_waiting, before_last)
    total = add_rows(xf, mean_ref[...], last_blocks)
    mean = (jnp.sum(total, axis=0, keepdims=True) / FIELD).astype(BF16)
    mean_ref[...] = jnp.broadcast_to(mean.astype(F32), (8, CIN))
    forward_others(xf, w, acc, xs, base, (1,))
    rest = head(acc, mean, w[TAPS], lab, wp, wc, cw, d, gp, gc, sp)

    bufs, sems = (d, sp, dbuf, sbuf), (ds_, dr)
    sent = []
    for i, (dz, late) in enumerate(ORDER):
        z2 = lax.rem(z + dz, 4)
        c2 = jnp.bitwise_xor(core, other_core(dz, late, z2))
        t = 4 * c2 + z2
        c = d_copies(i, share, t, device(xh, z2, c2, rep0), bufs, sems)
        flags = (wanted(0, t, share), wanted(1, t, share))
        sent.append((c, flags, t))
        pl.when(flags[0])(c[0].start)
        pl.when(flags[1])(c[1].start)
    rest()
    transpose_field(xf, xt)
    for c, _, t in sent:
        pl.when(t == NS - 1)(c[2].start)
    sibling = device(xh, z, 1 - core, rep0)

    def half(rows, plane):
        return pl.ds(pl.multiple_of(plane * rows, rows), rows)

    def proj_copy(j, from_ref, to_ref, target):
        return pltpu.make_async_remote_copy(
            from_ref, to_ref, ps.at[j], pr.at[j], device_id=target, device_id_type=MESH
        )

    to_sibling = (
        proj_copy(0, gp.at[half(4 * PROJ_SHARE, 1 - core)], gp_in, sibling),
        proj_copy(1, gc.at[half(4 * CLS_SHARE, 1 - core)], gc_in, sibling),
    )
    for c in to_sibling:
        c.start()

    lo, hi = share_taps(share)
    kb0, kb1 = branch_of(lo), branch_of(hi)
    pl.when(wanted(0, share, share))(lambda: shift_block(0, share, lambda j: d[kb0, j], dsh))
    pl.when(wanted(1, share, share))(lambda: shift_block(1, share, lambda j: d[kb1, j], dsh))

    def source(i):
        dz, late = pick(i, [o[0] for o in ORDER]), pick(i, [o[1] for o in ORDER])
        c2 = jnp.bitwise_xor(core, other_core(dz, late, z))
        z2 = lax.rem(z - dz + 4, 4)
        return 4 * c2 + z2, device(xh, z2, c2, rep0)

    def receive(i, _):
        block, dev = source(i)
        c = d_copies(i, block, share, dev, bufs, sems)
        for slot in range(2):

            @pl.when(wanted(slot, share, block))
            def _(slot=slot):
                c[slot].wait_recv()
                shift_block(slot, block, lambda j: dbuf[slot, block * ROWS_DEV + j], dsh)

        return 0

    for c in to_sibling:
        c.wait_recv()
    gp_sum[...] = (gp[half(4 * PROJ_SHARE, core), :].astype(F32) + gp_in[...].astype(F32)).astype(BF16)
    gc_sum[...] = (gc[half(4 * CLS_SHARE, core), :].astype(F32) + gc_in[...].astype(F32)).astype(BF16)
    far = far_first(z)
    lax.fori_loop(0, 3 + far, receive, 0)
    along_z = []
    for i, dz in enumerate((1, 3, 2)):
        z2 = lax.rem(z + dz, 4)
        target = device(xh, z2, core, rep0)
        along_z.append(proj_copy(2 + i, gp_sum.at[pl.ds(z2 * PROJ_SHARE, PROJ_SHARE)], pbuf.at[z], target))
        along_z.append(proj_copy(5 + i, gc_sum.at[pl.ds(z2 * CLS_SHARE, CLS_SHARE)], cbuf.at[z], target))
    weight_gradient(xt, dsh, acc_w, o_ref, jnp.bitwise_xor(core, far), True)
    lax.fori_loop(3 + far, NS - 1, receive, 0)
    for c in along_z:
        c.start()
    weight_gradient(xt, dsh, acc_w, o_ref, jnp.bitwise_xor(1 - core, far), False)
    pbuf[z] = gp_sum[pl.ds(pl.multiple_of(z * PROJ_SHARE, 32), PROJ_SHARE), :]
    cbuf[z] = gc_sum[pl.ds(pl.multiple_of(z * CLS_SHARE, 32), CLS_SHARE), :]
    sbuf[share] = sp[...]
    for i, dz in enumerate((1, 3, 2)):
        z2 = lax.rem(z - dz + 4, 4)
        proj_copy(2 + i, gp_sum.at[pl.ds(0, PROJ_SHARE)], pbuf.at[z2], sibling).wait_recv()
        proj_copy(5 + i, gc_sum.at[pl.ds(0, CLS_SHARE)], cbuf.at[z2], sibling).wait_recv()

    @pl.when(share == NS - 1)
    def _():
        @pl.loop(0, NS - 1)
        def _(i):
            block, dev = source(i)
            d_copies(i, block, share, dev, bufs, sems)[2].wait_recv()

    finish(o_ref, pbuf, cbuf, sbuf, mean_ref, share)
    drain()
    for c, flags, t in sent:
        pl.when(flags[0])(c[0].wait_send)
        pl.when(flags[1])(c[1].wait_send)
        pl.when(t == NS - 1)(c[2].wait_send)
    for c in to_sibling + tuple(along_z):
        c.wait_send()


def average(own, partner, own_tail, partner_tail, avg_in, avg_proj, avg_cls):
    avg_in[...] = (own[...].astype(F32) + partner[...].astype(F32)) * 0.5

    @pl.when(pl.program_id(0) == 0)
    def _():
        mean = (own_tail[...].astype(F32) + partner_tail[...].astype(F32)) * 0.5
        avg_proj[...] = mean[:PROJ_SHARE]
        by_class = mean[PROJ_SHARE:, :128].T
        for c in range(3):
            avg_cls[c] = by_class[c : c + 1, :]


def home(device_index, mask):
    sp, rep = device_index // 16, device_index % 16
    xh, z, core = sp // 4, sp % 4, rep % 2
    return (4 * core + z) * 16 + ((rep - core + xh) ^ mask)


def per_device(features, labels, w_in, w_proj, w_cls, class_weight, matching):
    x = features[0]
    vmem = pl.BlockSpec(memory_space=pltpu.VMEM)
    hbm = pl.BlockSpec(memory_space=pl.ANY)
    done = pl.pallas_call(
        kernel,
        out_shape=jax.ShapeDtypeStruct((OUT_ROWS, COUT), BF16),
        in_specs=[hbm, vmem, hbm, vmem, vmem, pl.BlockSpec(memory_space=pltpu.SMEM)],
        out_specs=vmem,
        scratch_shapes=[
            pltpu.VMEM((ROWS, COLS, CIN), BF16),
            pltpu.VMEM((29, CIN, COUT), BF16),
            pltpu.VMEM((4, PIX, COUT), F32),
            pltpu.VMEM((PIX, CIN), BF16),
            pltpu.VMEM((ROWS_DEV, 1, COLS), jnp.int32),
            pltpu.VMEM((4, ROWS_DEV, COLS, COUT), BF16),
            pltpu.VMEM((5 * COUT, COUT), BF16),
            pltpu.VMEM((COUT, 128), BF16),
            pltpu.VMEM((8, COUT), F32),
            pltpu.VMEM((8, CIN), F32),
            pltpu.VMEM((CIN, FIELD), BF16),
            pltpu.VMEM((2, ROWS, COLS, COUT), BF16),
            pltpu.VMEM((4 * PROJ_SHARE, COUT), BF16),
            pltpu.VMEM((4 * CLS_SHARE, 128), BF16),
            pltpu.VMEM((4 * PROJ_SHARE, COUT), BF16),
            pltpu.VMEM((4 * CLS_SHARE, 128), BF16),
            pltpu.VMEM((4, PROJ_SHARE, COUT), BF16),
            pltpu.VMEM((4, CLS_SHARE, 128), BF16),
            pltpu.VMEM((NS, 8, COUT), F32),
            pltpu.VMEM((5, ROWS, COLS, COUT), BF16),
            pltpu.VMEM((5, CIN, COUT), F32),
            pltpu.SemaphoreType.DMA((15,)),
            pltpu.SemaphoreType.DMA((15,)),
            pltpu.SemaphoreType.DMA((NS - 1, 3)),
            pltpu.SemaphoreType.DMA((NS - 1, 3)),
            pltpu.SemaphoreType.DMA((8,)),
            pltpu.SemaphoreType.DMA((8,)),
            pltpu.SemaphoreType.DMA,
            pltpu.SemaphoreType.DMA,
        ],
        compiler_params=pltpu.CompilerParams(collective_id=0, has_side_effects=True, vmem_limit_bytes=VMEM_LIMIT),
        name="field_gradient",
    )(x, labels.transpose(1, 0, 2), w_in, w_proj, w_cls.T, class_weight)

    def deliver(mask, value):
        n = lax.axis_size("rep") * lax.axis_size("space")
        own = lax.ppermute(value, ("space", "rep"), [(i, home(i, 0)) for i in range(n)])
        partner = lax.ppermute(value, ("space", "rep"), [(i, home(i, mask)) for i in range(n)])
        return own, partner

    own, partner = lax.switch(matching[0] - 1, [functools.partial(deliver, m) for m in range(1, 16)], done)

    steps = 2
    main = pl.BlockSpec((SHARE // steps, COUT), lambda i: (i, 0))
    tail = pl.BlockSpec((pl.Element(OUT_ROWS - SHARE), pl.Element(COUT)), lambda i: (SHARE, 0))
    avg_in, avg_proj, avg_cls = pl.pallas_call(
        average,
        grid=(steps,),
        out_shape=(
            jax.ShapeDtypeStruct((SHARE, COUT), F32),
            jax.ShapeDtypeStruct((PROJ_SHARE, COUT), F32),
            jax.ShapeDtypeStruct((3, 1, CLS_SHARE), F32),
        ),
        in_specs=[main, main, tail, tail],
        out_specs=(
            main,
            pl.BlockSpec((PROJ_SHARE, COUT), lambda i: (0, 0)),
            pl.BlockSpec((3, 1, CLS_SHARE), lambda i: (0, 0, 0)),
        ),
        name="average",
    )(own, partner, own, partner)
    return avg_in[None], avg_proj[None], avg_cls.transpose(1, 2, 0)


def solution(mesh):
    return jax.shard_map(
        per_device,
        mesh=mesh,
        in_specs=(P("rep", "space", None, None), P("rep", "space", None), P(), P(), P(), P(), P()),
        out_specs=(P("rep", "space", None), P("rep", "space", None), P("rep", "space", None)),
        check_vma=False,
    )
```
